32 devices in a mesh: fsdp: 8 (over z, x), tensor: 4 (over y, core).
Axes of the slice: x: 2, y: 2, z: 4, core: 2. Of those that a mesh axis runs over, the one named last changes fastest.
Arguments:
- inputs: float32 [16384, 768], P(('fsdp', 'tensor')), may hold values from -10 to 10
- qkv_weight: bfloat16 [3, 768, 768], P(None, 'fsdp', 'tensor'), may hold values from -0.21875 to 0.21875
- out_weight: bfloat16 [768, 768], P('tensor', 'fsdp'), may hold values from -0.4375 to 0.4375
- conv_weight: float32 [12, 33], replicated, may hold values from -1 to 1
- up_weight: bfloat16 [768, 3072], P('fsdp', 'tensor'), may hold values from -0.21875 to 0.21875
- down_weight: bfloat16 [3072, 768], P('tensor', 'fsdp'), may hold values from -0.109375 to 0.109375
- mix_gain: float32 [768], replicated, may hold values from 0.25 to 1.75
- mix_bias: float32 [768], replicated, may hold values from -1.2 to 1.2
- feed_gain: float32 [768], replicated, may hold values from 0.25 to 1.75
- feed_bias: float32 [768], replicated, may hold values from -1.2 to 1.2
- out_grad: float32 [16384, 768], P(('fsdp', 'tensor')), may hold values from -6 to 6
Outputs:
- output: float32 [16384, 768], P(('fsdp', 'tensor'))
- input_grad: float32 [16384, 768], P(('fsdp', 'tensor'))
- qkv_grad: float32 [3, 768, 768], P(None, 'fsdp', 'tensor')
- out_weight_grad: float32 [768, 768], P('tensor', 'fsdp')
- conv_grad: float32 [12, 33], replicated
- up_grad: float32 [768, 3072], P('fsdp', 'tensor')
- down_grad: float32 [3072, 768], P('tensor', 'fsdp')
- mix_gain_grad: float32 [768], replicated
- mix_bias_grad: float32 [768], replicated
- feed_gain_grad: float32 [768], replicated
- feed_bias_grad: float32 [768], replicated
The draws below stay inside these ranges and needn't reach their ends.
All inputs are finite; a program needn't handle non-finite values.
Results may differ from the reference program's by a relative error of at most 0.014.
Values may be sent and summed in bfloat16 or wider, within the bound.
No kernel may reach another device: no remote copies, remote signals or barrier semaphores. Data moves between devices by JAX's collectives and lax.ppermute only.
A program may use at most 192 MiB of HBM per device.

```python
import math
import jax
import jax.numpy as jnp
from jax import lax

D = 768
HEADS = 12
HD = 64
FF = 3072
LANDMARKS = 64
KW = 33
ITERS = 6
LEN = 2048
TOKENS = 16384


def draw_inputs(key, part):
    sequences = TOKENS // LEN
    segment_len = LEN // LANDMARKS
    key_scale, key_shared, key_rough = jax.random.split(key, 3)
    factor = jnp.exp(jax.random.uniform(key_scale, (sequences, 1, 1, 1), jnp.float32, math.log(0.8), math.log(1.25)))
    shared = jnp.clip(jax.random.normal(key_shared, (sequences, LANDMARKS, 1, D), jnp.float32), -4.0, 4.0)
    rough = jnp.clip(jax.random.normal(key_rough, (sequences, LANDMARKS, segment_len, D), jnp.float32), -4.0, 4.0)
    values = 1.3 * factor * shared + 0.8 * rough
    return values.reshape(TOKENS, D)


def level_of(own_key, shape, cuts, smallest, high):
    loudness = 1.0
    for axis_at, shards_of in cuts:
        draws = jax.random.uniform(jax.random.fold_in(jax.random.fold_in(own_key, 6), axis_at), (shards_of,), jnp.float32, smallest / len(cuts), high / len(cuts))
        loudness = loudness * jnp.repeat(jnp.exp(draws), shape[axis_at] // shards_of).reshape((-1,) + (1,) * (len(shape) - 1 - axis_at))
    return loudness


def gaussian(own_key, shape, scale, most, shards=(), kind=jnp.bfloat16):
    drawn = scale * jax.random.normal(own_key, shape, jnp.float32)
    if shards:
        drawn = drawn * level_of(own_key, shape, shards, -0.22, 0.18)
    return jnp.clip(drawn, -most, most).astype(kind)


def setup_inputs(seed: int = 0) -> dict:
    keys = jax.random.split(jax.random.key(seed), 12)
    inputs = draw_inputs(jax.random.fold_in(keys[11], 71), 0)
    qkv_weight = gaussian(keys[1], (3, D, D), D ** -0.5, 0.21875, ((1, 8), (2, 4)))
    out_weight = gaussian(keys[2], (D, D), (D // 4) ** -0.5, 0.4375, ((0, 4), (1, 8)))
    conv_weight = gaussian(keys[3], (HEADS, KW), KW ** -0.5, 1.0, (), jnp.float32)
    up_weight = gaussian(keys[4], (D, FF), D ** -0.5, 0.21875, ((0, 8), (1, 4)))
    down_weight = gaussian(keys[5], (FF, D), FF ** -0.5, 0.109375, ((0, 4), (1, 8)))
    mix_gain = jnp.clip(1.0 + 0.15 * jax.random.normal(keys[6], (D,), jnp.float32), 0.25, 1.75)
    mix_bias = gaussian(keys[7], (D,), 0.3, 1.2, (), jnp.float32)
    feed_gain = jnp.clip(1.0 + 0.15 * jax.random.normal(keys[8], (D,), jnp.float32), 0.25, 1.75)
    feed_bias = gaussian(keys[9], (D,), 0.3, 1.2, (), jnp.float32)
    out_grad = gaussian(keys[10], (TOKENS, D), 1.0, 6.0, ((0, 32),), jnp.float32)
    return {"inputs": inputs, "qkv_weight": qkv_weight, "out_weight": out_weight, "conv_weight": conv_weight, "up_weight": up_weight, "down_weight": down_weight, "mix_gain": mix_gain, "mix_bias": mix_bias, "feed_gain": feed_gain, "feed_bias": feed_bias, "out_grad": out_grad}


@jax.custom_vjp
def low(v):
    return lax.optimization_barrier(v.astype(jnp.bfloat16)).astype(jnp.float32)

@jax.custom_vjp
def low_back(v):
    return v

def low_keep(v):
    return (low(v), None)

def low_pass(kept, grad):
    return (grad,)

def back_keep(v):
    return (v, None)

def back_low(kept, grad):
    return (low(grad),)
low.defvjp(low_keep, low_pass)
low_back.defvjp(back_keep, back_low)

def landmarks(query, key):
    heads, length, width = query.shape
    factor = width ** (-0.25)
    scaled_q = query * factor
    scaled_k = key * factor
    marks_q = lax.optimization_barrier(jnp.mean(scaled_q.reshape(heads, LANDMARKS, length // LANDMARKS, width), axis=2))
    marks_k = lax.optimization_barrier(jnp.mean(scaled_k.reshape(heads, LANDMARKS, length // LANDMARKS, width), axis=2))
    inner = jnp.einsum('hid,hjd->hij', marks_q, marks_k, precision=lax.Precision.HIGHEST)
    kernel_two = jax.nn.softmax(inner, axis=-1)
    return (scaled_q, scaled_k, marks_q, marks_k, kernel_two)

def column_peak(query, key):
    kernel_two = landmarks(query, key)[4]
    return lax.optimization_barrier(jnp.max(lax.optimization_barrier(jnp.sum(kernel_two, axis=1)), axis=1))

def mixing(query, key, value, conv, inverse):
    high = lax.Precision.HIGHEST
    scaled_q, scaled_k, marks_q, marks_k, kernel_two = landmarks(query, key)
    length = query.shape[1]
    kernel_one = jax.nn.softmax(jnp.einsum('hnd,hjd->hnj', scaled_q, marks_k, precision=high), axis=-1)
    kernel_three = jax.nn.softmax(jnp.einsum('hid,hnd->hin', marks_q, scaled_k, precision=high), axis=-1)
    approx = jnp.swapaxes(kernel_two, 1, 2) * inverse[:, None, None]
    ident = jnp.eye(kernel_two.shape[1], dtype=jnp.float32)
    for step in range(ITERS):
        prod = jnp.einsum('hij,hjk->hik', kernel_two, approx, precision=high)
        inner = 7.0 * ident - prod
        inner = 15.0 * ident - jnp.einsum('hij,hjk->hik', prod, inner, precision=high)
        inner = 13.0 * ident - jnp.einsum('hij,hjk->hik', prod, inner, precision=high)
        approx = jnp.einsum('hij,hjk->hik', 0.25 * approx, inner, precision=high)
    summary = jnp.einsum('hin,hnd->hid', kernel_three, value, precision=high)
    carried = jnp.einsum('hij,hjd->hid', approx, summary, precision=high)
    mixed = jnp.einsum('hnj,hjd->hnd', kernel_one, carried, precision=high)
    margin = conv.shape[1] // 2
    padded = jnp.pad(value, ((0, 0), (margin, margin), (0, 0)))
    for tap in range(conv.shape[1]):
        mixed = mixed + conv[:, tap][:, None, None] * padded[:, tap:tap + length, :]
    return mixed

def layer_norm(rows, gain, shift):
    center = rows - lax.optimization_barrier(jnp.mean(rows, axis=-1, keepdims=True))
    spread = lax.optimization_barrier(jnp.mean(center * center, axis=-1, keepdims=True))
    return center * lax.rsqrt(spread + 1e-05) * gain + shift

def forward(inputs, qkv_weight, out_weight, conv_weight, up_weight, down_weight, mix_gain, mix_bias, feed_gain, feed_bias):
    high = lax.Precision.HIGHEST
    count = inputs.shape[0] // LEN
    rounded = low(inputs)
    qkv = low_back(jnp.einsum('nd,kdc->knc', rounded, qkv_weight, precision=high, preferred_element_type=jnp.float32))

    def split_heads(block):
        return block.reshape(count, LEN, HEADS, HD).transpose(0, 2, 1, 3)
    query, key, value = (split_heads(qkv[0]), split_heads(qkv[1]), split_heads(qkv[2]))
    peaks = jax.vmap(column_peak)(query, key)
    inverse = 1.0 / lax.optimization_barrier(jnp.max(peaks, axis=0))
    mixed = jax.vmap(mixing, in_axes=(0, 0, 0, None, None))(query, key, value, conv_weight, inverse)
    context = mixed.transpose(0, 2, 1, 3).reshape(count * LEN, D)
    attended = low_back(jnp.dot(low(context), out_weight, precision=high, preferred_element_type=jnp.float32))
    mixed_rows = layer_norm(inputs + attended, mix_gain, mix_bias)
    up = low_back(jnp.dot(low(mixed_rows), up_weight, precision=high, preferred_element_type=jnp.float32))
    act = jax.nn.gelu(up, approximate=True)
    down = low_back(jnp.dot(low(act), down_weight, precision=high, preferred_element_type=jnp.float32))
    return layer_norm(mixed_rows + down, feed_gain, feed_bias)

def reference(inputs, qkv_weight, out_weight, conv_weight, up_weight, down_weight, mix_gain, mix_bias, feed_gain, feed_bias, out_grad):
    params = (inputs, qkv_weight.astype(jnp.float32), out_weight.astype(jnp.float32), conv_weight, up_weight.astype(jnp.float32), down_weight.astype(jnp.float32), mix_gain, mix_bias, feed_gain, feed_bias)
    output, pullback = jax.vjp(forward, *params)
    grads = pullback(out_grad)
    return (output, grads[0], grads[1], grads[2], grads[3], grads[4], grads[5], grads[6], grads[7], grads[8], grads[9])
```

```python
import jax
import jax.numpy as jnp
from jax import lax
from jax.experimental import pallas as pl
from jax.experimental.pallas import tpu as pltpu
from jax.sharding import PartitionSpec as P
HD=64; LANDMARKS=64; ITERS=6
F32=jnp.float32; BF=jnp.bfloat16
SPAN=256; REACH=128

def dot(a,b,ca,cb):
    return lax.dot_general(a,b,(((ca,),(cb,)),((),())),preferred_element_type=F32)

def low(a):
    return a.astype(BF)

def parts(a):
    high=a.astype(BF)
    return high,(a-high.astype(F32)).astype(BF)

def dot3(a,b,ca,cb):
    ah,al=a if isinstance(a,tuple) else parts(a)
    bh,bl=b if isinstance(b,tuple) else parts(b)
    return dot(ah,bh,ca,cb)+(dot(ah,bl,ca,cb)+dot(al,bh,ca,cb))

def segments(length):
    row=lax.broadcasted_iota(jnp.int32,(LANDMARKS,length),0)
    col=lax.broadcasted_iota(jnp.int32,(LANDMARKS,length),1)
    size=length//LANDMARKS
    first=row*size
    return jnp.where((col>=first)&(col<first+size),1.0,0.0).astype(BF)

def soft_rows(s):
    e=jnp.exp(s-jnp.max(s,axis=1,keepdims=True))
    return e*(1.0/jnp.sum(e,axis=1,keepdims=True))

def soft_cols(s):
    e=jnp.exp(s-jnp.max(s,axis=0,keepdims=True))
    return e*(1.0/jnp.sum(e,axis=0,keepdims=True))

def head(ref,h):
    return ref[h*HD:(h+1)*HD,:]

def marks_body(qkv_ref,marks_ref,k2_ref,peak_ref):
    heads=k2_ref.shape[0]
    length=qkv_ref.shape[2]
    seg=segments(length)
    factor=HD**-0.25
    scale=factor/(length//LANDMARKS)
    peak_ref[...]=jnp.zeros(peak_ref.shape,F32)
    for h in range(heads):
        rows=slice(h*HD,(h+1)*HD)
        found=[]
        for j in range(2):
            x=qkv_ref[j,rows,:]
            xh,xl=parts(x)
            m=(dot(seg,xh,1,1)+dot(seg,xl,1,1))*scale
            marks_ref[h,j]=m
            found.append(m)
        inner=dot3(found[0],found[1],1,1)
        k2=soft_rows(inner)
        k2_ref[h]=k2
        top=jnp.max(jnp.sum(k2,axis=0,keepdims=True),axis=1,keepdims=True)
        peak_ref[h:h+1,:]=jnp.broadcast_to(top,(1,128))

def band(taps_row):
    wide=jnp.broadcast_to(taps_row,(SPAN,taps_row.shape[1]))
    return pltpu.roll(wide,0,1,stride=1,stride_axis=0)

def windows(pad_ref,x,length):
    pad_ref[:,:REACH]=jnp.zeros((HD,REACH),BF)
    pad_ref[:,REACH+length:]=jnp.zeros((HD,REACH),BF)
    pad_ref[:,REACH:REACH+length]=low(x)
    return jnp.concatenate([pad_ref[:,b*SPAN:b*SPAN+SPAN+2*REACH] for b in range(length//SPAN)],axis=0)

def kernels_body(qkv_ref,marks_ref,taps_ref,k1_ref,k3_ref,sum_ref,conv_ref,pad_ref):
    length=qkv_ref.shape[2]
    factor=HD**-0.25
    ql=marks_ref[0,0]; kl=marks_ref[0,1]
    k1_ref[...]=soft_cols(dot3(kl,qkv_ref[0]*factor,1,0))
    k3=soft_rows(dot3(ql,qkv_ref[1]*factor,1,0))
    k3_ref[...]=k3
    v=qkv_ref[2]
    sum_ref[0]=dot(low(k3),low(v),1,1)
    wins=windows(pad_ref,v,length)
    out=dot(wins,low(band(taps_ref[0,0:1,:])),1,1)
    for b in range(length//SPAN):
        conv_ref[:,b*SPAN:(b+1)*SPAN]=out[b*HD:(b+1)*HD,:]

def eye():
    r=lax.broadcasted_iota(jnp.int32,(LANDMARKS,LANDMARKS),0)
    c=lax.broadcasted_iota(jnp.int32,(LANDMARKS,LANDMARKS),1)
    return jnp.where(r==c,1.0,0.0)

def mix_body(k2_ref,peak_ref,sum_ref,k1_ref,conv_ref,ctx_ref,hist_ref,fin_ref):
    heads=k2_ref.shape[0]
    ident=eye()
    k2=[k2_ref[h] for h in range(heads)]
    k2p=[parts(x) for x in k2]
    a=[k2[h].T*(1.0/peak_ref[h:h+1,0:1]) for h in range(heads)]
    for step in range(ITERS):
        ap=[parts(x) for x in a]
        p=[dot3(k2p[h],ap[h],1,0) for h in range(heads)]
        pp=[parts(x) for x in p]
        t=[15.0*ident-dot3(pp[h],7.0*ident-p[h],1,0) for h in range(heads)]
        u=[13.0*ident-dot3(pp[h],t[h],1,0) for h in range(heads)]
        for h in range(heads):
            hist_ref[h,step,0]=a[h]; hist_ref[h,step,1]=p[h]
            hist_ref[h,step,2]=t[h]; hist_ref[h,step,3]=u[h]
        a=[0.25*dot3(ap[h],u[h],1,0) for h in range(heads)]
    for h in range(heads):
        car=dot3(a[h],sum_ref[h],1,0)
        fin_ref[h,0]=a[h]; fin_ref[h,1]=car
        rows=slice(h*HD,(h+1)*HD)
        ctx_ref[rows,:]=(dot(low(car),low(k1_ref[rows,:]),0,0)+conv_ref[rows,:]).astype(BF)

def back_marks_body(g_ref,k1_ref,k2_ref,peak_ref,sum_ref,hist_ref,fin_ref,vwin_ref,dsum_ref,dk2_ref,dinv_ref,dtap_ref,pad_ref,gst_ref):
    heads=k2_ref.shape[0]
    length=g_ref.shape[1]
    ident=eye()
    dinv_ref[...]=jnp.zeros(dinv_ref.shape,F32)
    dtap_ref[...]=jnp.zeros(dtap_ref.shape,F32)
    k2p=[parts(k2_ref[h]) for h in range(heads)]
    da=[]
    for h in range(heads):
        rows=slice(h*HD,(h+1)*HD)
        dcar=dot(low(k1_ref[rows,:]),g_ref[rows,:],1,1)
        dp_=parts(dcar)
        da.append(dot3(dp_,sum_ref[h],1,1))
        dsum_ref[h]=dot3(fin_ref[h,0],dp_,0,0)
    dk2=[None]*heads
    for step in reversed(range(ITERS)):
        nxt=[]
        for h in range(heads):
            A=parts(hist_ref[h,step,0]); P=hist_ref[h,step,1]; T2=hist_ref[h,step,2]; T3=hist_ref[h,step,3]
            Pp=parts(P); D=parts(da[h])
            dT3=0.25*dot3(A,D,0,0)
            dAn=0.25*dot3(D,T3,1,1)
            d3=parts(dT3)
            dT2=-dot3(Pp,d3,0,0)
            d2=parts(dT2)
            dP=-dot3(d3,T2,1,1)-dot3(d2,7.0*ident-P,1,1)+dot3(Pp,d2,0,0)
            dPp=parts(dP)
            add=dot3(dPp,A,1,1)
            dk2[h]=add if dk2[h] is None else dk2[h]+add
            nxt.append(dAn+dot3(k2p[h],dPp,0,0))
        da=nxt
    for h in range(heads):
        inv=1.0/peak_ref[h:h+1,0:1]
        dk2_ref[h]=dk2[h]+da[h].T*inv
        prod=da[h]*k2_ref[h].T
        tot=jnp.sum(jnp.sum(prod,axis=0,keepdims=True),axis=1,keepdims=True)
        dinv_ref[h:h+1,:]=jnp.broadcast_to(tot,(1,128))
    width=SPAN+2*REACH
    r=lax.broadcasted_iota(jnp.int32,(SPAN,SPAN),0)
    c=lax.broadcasted_iota(jnp.int32,(SPAN,SPAN),1)
    flip=jnp.where(r+c==SPAN-1,1.0,0.0).astype(BF)
    for h in range(heads):
        wins=windows(pad_ref,vwin_ref[0,h*HD:(h+1)*HD,:],length)
        for b in range(length//SPAN):
            gst_ref[b*HD:(b+1)*HD,:]=g_ref[h*HD:(h+1)*HD,b*SPAN:(b+1)*SPAN]
        m=dot(low(dot(gst_ref[...],flip,1,0)),wins,0,0)
        m=pltpu.roll(m,0,1,stride=1,stride_axis=0)
        s=jnp.sum(m,axis=0,keepdims=True)
        dtap_ref[h:h+1,:]=s

def back_body(qkv_ref,g_ref,marks_ref,k1_ref,k3_ref,sum_ref,fin_ref,dsum_ref,taps_ref,dqs_ref,dks_ref,dv_ref,dmarks_ref,pad_ref):
    length=qkv_ref.shape[2]
    factor=HD**-0.25
    g=g_ref[...]
    car=low(fin_ref[0,1]); dsum=dsum_ref[0]
    k1=k1_ref[...]
    dk1=dot(car,g,1,0)
    ds1=low(k1*(dk1-jnp.sum(k1*dk1,axis=0,keepdims=True)))
    dqs_ref[...]=dot(low(marks_ref[0,1]),ds1,0,0)
    dmarks_ref[0,1]=dot(ds1,low(qkv_ref[0]*factor),1,1)
    k3=k3_ref[...]
    v=qkv_ref[2]
    dl=low(dsum)
    delta=jnp.sum(dsum*sum_ref[0],axis=1,keepdims=True)
    ds3=low(k3*(dot(dl,low(v),1,0)-delta))
    dks_ref[...]=dot(low(marks_ref[0,0]),ds3,0,0)
    dmarks_ref[0,0]=dot(ds3,low(qkv_ref[1]*factor),1,1)
    wins=windows(pad_ref,g,length)
    out=dot(wins,low(band(taps_ref[0,1:2,:])),1,1)
    dv=dot(dl,low(k3),0,0)
    for b in range(length//SPAN):
        dv_ref[:,b*SPAN:(b+1)*SPAN]=(dv[:,b*SPAN:(b+1)*SPAN]+out[b*HD:(b+1)*HD,:]).astype(BF)

def close_body(k2_ref,dk2_ref,own_ref,marks_ref,dmarks_ref,dqs_ref,dks_ref,dv_ref,out_ref):
    heads=k2_ref.shape[0]
    length=dqs_ref.shape[1]
    factor=HD**-0.25
    seg=segments(length)
    scale=factor/(length//LANDMARKS)
    for h in range(heads):
        rows=slice(h*HD,(h+1)*HD)
        k2=k2_ref[h]
        sums=jnp.sum(k2,axis=0,keepdims=True)
        hit=jnp.where(sums==jnp.max(sums,axis=1,keepdims=True),1.0,0.0)
        hit=hit*(1.0/jnp.sum(hit,axis=1,keepdims=True))
        dk2=dk2_ref[h]+hit*own_ref[h:h+1,0:1]
        ds2=k2*(dk2-jnp.sum(k2*dk2,axis=1,keepdims=True))
        dp=parts(ds2)
        dql=dmarks_ref[h,0]+dot3(dp,marks_ref[h,1],1,0)
        dkl=dmarks_ref[h,1]+dot3(dp,marks_ref[h,0],0,0)
        for j,(d,s_ref) in enumerate(((dql,dqs_ref),(dkl,dks_ref))):
            dh,dl=parts(d*scale)
            spread=dot(dh,seg,0,0)+dot(dl,seg,0,0)
            out_ref[j,rows,:]=(s_ref[rows,:]*factor+spread).astype(BF)
        out_ref[2,rows,:]=dv_ref[rows,:]

def tap_rows(conv):
    heads,count=conv.shape
    width=SPAN+2*REACH
    left=REACH-count//2
    pad=((0,0),(left,width-left-count))
    return jnp.stack([jnp.pad(conv,pad),jnp.pad(conv[:,::-1],pad)],axis=1)

VM=pl.BlockSpec(memory_space=pltpu.VMEM)
def sds(shape,dt=F32): return jax.ShapeDtypeStruct(shape,dt)
LIM=56*2**20
def params(): return pltpu.CompilerParams(vmem_limit_bytes=LIM)

def marks_call(qkv,heads):
    n=qkv.shape[2]
    return pl.pallas_call(marks_body,out_shape=(sds((heads,2,LANDMARKS,HD)),sds((heads,LANDMARKS,LANDMARKS)),sds((8,128))),
        in_specs=[pl.BlockSpec((2,heads*HD,n),lambda i:(0,0,0))],grid=(1,),
        out_specs=(pl.BlockSpec((heads,2,LANDMARKS,HD),lambda i:(0,0,0,0)),pl.BlockSpec((heads,LANDMARKS,LANDMARKS),lambda i:(0,0,0)),pl.BlockSpec((8,128),lambda i:(0,0))),
        name="marks",compiler_params=params())(qkv)

def kernels_call(qkv,marks,taps,heads):
    n=qkv.shape[2]
    row=lambda: pl.BlockSpec((HD,n),lambda h:(h,0))
    return pl.pallas_call(kernels_body,grid=(heads,),
        in_specs=[pl.BlockSpec((3,HD,n),lambda h:(0,h,0)),pl.BlockSpec((1,2,LANDMARKS,HD),lambda h:(h,0,0,0)),pl.BlockSpec((1,2,taps.shape[2]),lambda h:(h,0,0))],
        out_specs=(row(),row(),pl.BlockSpec((1,LANDMARKS,HD),lambda h:(h,0,0)),row()),
        out_shape=(sds((heads*HD,n)),sds((heads*HD,n)),sds((heads,LANDMARKS,HD)),sds((heads*HD,n))),
        scratch_shapes=[pltpu.VMEM((HD,n+2*REACH),BF)],name="kernels",compiler_params=params())(qkv,marks,taps)

def mix_call(k2,peak,summ,k1,conv,heads):
    n=k1.shape[1]
    return pl.pallas_call(mix_body,in_specs=[VM]*5,out_specs=(VM,VM,VM),
        out_shape=(sds((heads*HD,n),BF),sds((heads,ITERS,4,LANDMARKS,LANDMARKS)),sds((heads,2,LANDMARKS,LANDMARKS))),
        name="mix",compiler_params=params())(k2,peak,summ,k1,conv)

def back_marks_call(g,k1,k2,peak,summ,hist,fin,qkv,heads):
    n=g.shape[1]
    z=lambda r:(lambda i:(0,)*r)
    full=lambda s: pl.BlockSpec(s,z(len(s)))
    return pl.pallas_call(back_marks_body,grid=(1,),
        in_specs=[full(g.shape),full(k1.shape),full(k2.shape),full(peak.shape),full(summ.shape),full(hist.shape),full(fin.shape),pl.BlockSpec((1,heads*HD,n),lambda i:(2,0,0))],
        out_specs=(full((heads,LANDMARKS,HD)),full((heads,LANDMARKS,LANDMARKS)),full((8,128)),full((8,SPAN+2*REACH))),
        out_shape=(sds((heads,LANDMARKS,HD)),sds((heads,LANDMARKS,LANDMARKS)),sds((8,128)),sds((8,SPAN+2*REACH))),
        scratch_shapes=[pltpu.VMEM((HD,n+2*REACH),BF),pltpu.VMEM((n//SPAN*HD,SPAN),BF)],
        name="back_marks",compiler_params=params())(g,k1,k2,peak,summ,hist,fin,qkv)

def back_call(qkv,g,marks,k1,k3,summ,fin,dsum,taps,heads):
    n=g.shape[1]
    row=lambda: pl.BlockSpec((HD,n),lambda h:(h,0))
    sq=lambda: pl.BlockSpec((1,LANDMARKS,HD),lambda h:(h,0,0))
    two=lambda: pl.BlockSpec((1,2,LANDMARKS,HD),lambda h:(h,0,0,0))
    return pl.pallas_call(back_body,grid=(heads,),
        in_specs=[pl.BlockSpec((3,HD,n),lambda h:(0,h,0)),row(),two(),row(),row(),sq(),two(),sq(),pl.BlockSpec((1,2,taps.shape[2]),lambda h:(h,0,0))],
        out_specs=(row(),row(),row(),two()),
        out_shape=(sds((heads*HD,n)),sds((heads*HD,n)),sds((heads*HD,n),BF),sds((heads,2,LANDMARKS,HD))),
        scratch_shapes=[pltpu.VMEM((HD,n+2*REACH),BF)],name="back",compiler_params=params())(qkv,g,marks,k1,k3,summ,fin,dsum,taps)

def close_call(k2,dk2,own,marks,dmarks,dqs,dks,dv,heads):
    n=dqs.shape[1]
    return pl.pallas_call(close_body,in_specs=[VM]*8,out_specs=VM,out_shape=sds((3,heads*HD,n),BF),
        name="close",compiler_params=params())(k2,dk2,own,marks,dmarks,dqs,dks,dv)


def xor_pairs(size, bit):
    return [(i, i ^ bit) for i in range(size)]


def xor_swap(value, axis, bit):
    return lax.ppermute(value, axis, xor_pairs(lax.axis_size(axis), bit))


def power_of_two(size):
    return size & (size - 1) == 0


def everywhere(value, axis, combine, plain):
    size = lax.axis_size(axis)
    if not power_of_two(size):
        return plain(value, axis)
    bit = 1
    while bit < size:
        value = combine(value, xor_swap(value, axis, bit))
        bit *= 2
    return value


def sum_everywhere(value, axis):
    return everywhere(value, axis, jnp.add, lax.psum)


def gather_near(value):
    far = xor_swap(value, "tensor", 2)
    near = xor_swap(value, "tensor", 1)
    last = xor_swap(far, "tensor", 1)
    return jnp.concatenate([value, near, far, last], axis=0)


def scatter_near(value):
    rows = value.shape[0] // 4
    block = lambda j: value[j * rows : (j + 1) * rows]
    far = xor_swap(jnp.concatenate([block(3)], axis=0), "tensor", 1)
    near = xor_swap(block(1), "tensor", 1)
    sent = block(2).astype(F32) + far.astype(F32)
    got = xor_swap(sent.astype(BF), "tensor", 2)
    return block(0).astype(F32) + near.astype(F32) + got.astype(F32)


def reorder(value, axis):
    place = lax.axis_index("tensor")
    rows = value.shape[axis] // 4
    return jnp.concatenate(
        [lax.dynamic_slice_in_dim(value, (place ^ j) * rows, rows, axis) for j in range(4)], axis=axis
    )


def sum_at_owner(value, rows):
    count = lax.axis_size("fsdp")
    tiles = value.reshape(count, rows, *value.shape[1:])
    arrived = lax.all_to_all(tiles, "fsdp", split_axis=0, concat_axis=0, tiled=True)
    return arrived.astype(F32).sum(axis=0)


def gelu_tanh(value):
    return jax.nn.gelu(value, approximate=True)


def norm_forward(rows, gain, shift):
    center = rows - jnp.mean(rows, axis=-1, keepdims=True)
    spread = jnp.mean(center * center, axis=-1, keepdims=True)
    factor = lax.rsqrt(spread + 1e-05)
    normed = center * factor
    return (normed * gain + shift, normed, factor)


def norm_backward(cotan, normed, factor, gain):
    scaled = cotan * gain
    return factor * (
        scaled
        - jnp.mean(scaled, axis=-1, keepdims=True)
        - normed * jnp.mean(scaled * normed, axis=-1, keepdims=True)
    )


def norm_params(cotan, normed):
    return (jnp.sum(cotan * normed, axis=0), jnp.sum(cotan, axis=0))


def mul(spec, a, b, kind=F32):
    return jnp.einsum(spec, a, b, preferred_element_type=F32).astype(kind)


def shards(
    inputs,
    qkv_weight,
    out_weight,
    conv_weight,
    up_weight,
    down_weight,
    mix_gain,
    mix_bias,
    feed_gain,
    feed_bias,
    out_grad,
):
    place = lax.axis_index("tensor")
    columns = qkv_weight.shape[2]
    heads = columns // HD
    units = up_weight.shape[1]
    share = qkv_weight.shape[1]
    gathered_in = reorder(gather_near(inputs.astype(BF)), 0)
    w_qkv = lax.all_gather(qkv_weight, "fsdp", axis=1, tiled=True)
    packed = jnp.concatenate([up_weight, down_weight.T, out_weight.T], axis=1)
    w_rest = lax.all_gather(packed, "fsdp", axis=0, tiled=True)
    w_up = w_rest[:, :units]
    w_down = w_rest[:, units : 2 * units]
    w_out = w_rest[:, 2 * units :]
    qkv = mul("nd,kdc->kcn", gathered_in, w_qkv)
    conv_local = lax.dynamic_slice_in_dim(conv_weight, place * heads, heads, 0)
    taps = tap_rows(conv_local)
    marks, k2, peak_local = marks_call(qkv, heads)
    peak = everywhere(peak_local, "fsdp", jnp.maximum, lax.pmax)
    k1, k3, summary, conv = kernels_call(qkv, marks, taps, heads)
    context, hist, fin = mix_call(k2, peak, summary, k1, conv, heads)
    context_own = reorder(context, 1)
    attended = scatter_near(mul("cn,dc->nd", context_own, w_out, BF))
    mixed_rows, normed_mix, factor_mix = norm_forward(inputs + attended, mix_gain, mix_bias)
    mixed_low = gather_near(mixed_rows.astype(BF))
    up_rows = mul("nd,df->nf", mixed_low, w_up)
    act, gelu_back = jax.vjp(gelu_tanh, up_rows)
    act_low = act.astype(BF)
    fed = scatter_near(mul("nf,df->nd", act_low, w_down, BF))
    output, normed_feed, factor_feed = norm_forward(mixed_rows + fed, feed_gain, feed_bias)
    grad_feed = norm_backward(out_grad, normed_feed, factor_feed, feed_gain)
    feed_gain_part, feed_bias_part = norm_params(out_grad, normed_feed)
    grad_down = gather_near(grad_feed.astype(BF))
    grad_act = mul("nd,df->nf", grad_down, w_down)
    grad_up = gelu_back(grad_act)[0].astype(BF)
    grad_mixed_rows = grad_feed + scatter_near(mul("nf,df->nd", grad_up, w_up, BF))
    down_share = sum_at_owner(mul("nd,nf->df", grad_down, act_low, BF), share).T
    up_share = sum_at_owner(mul("nd,nf->df", mixed_low, grad_up, BF), share)
    grad_mix = norm_backward(grad_mixed_rows, normed_mix, factor_mix, mix_gain)
    mix_gain_part, mix_bias_part = norm_params(grad_mixed_rows, normed_mix)
    grad_attended = gather_near(grad_mix.astype(BF))
    out_share = sum_at_owner(mul("nd,cn->dc", grad_attended, context_own, BF), share).T
    grad_context = reorder(mul("nd,dc->cn", grad_attended, w_out, BF), 1)
    dsum, dk2, dinv, dtap = back_marks_call(grad_context, k1, k2, peak, summary, hist, fin, qkv, heads)
    first = SPAN - 1 + REACH - conv_weight.shape[1] // 2
    dtap = dtap[:, first : first + 128]
    norm_stack = jnp.stack([mix_gain_part, mix_bias_part, feed_gain_part, feed_bias_part])
    norm_rows = norm_stack.reshape(-1, 128)
    total = sum_everywhere(jnp.concatenate([dinv, dtap, norm_rows], axis=0), "fsdp")
    own = jnp.where(peak_local == peak, -total[:8] / (peak * peak), 0.0)
    dqs, dks, dv, dmarks = back_call(qkv, grad_context, marks, k1, k3, summary, fin, dsum, taps, heads)
    grad_qkv = close_call(k2, dk2, own, marks, dmarks, dqs, dks, dv, heads)
    conv_full = lax.dynamic_update_slice_in_dim(
        jnp.zeros((conv_weight.shape[0], 128), F32), total[8 : 8 + heads], place * heads, 0
    )
    total = sum_everywhere(jnp.concatenate([conv_full, total[16:]], axis=0), "tensor")
    conv_grad = total[: conv_weight.shape[0], : conv_weight.shape[1]]
    norm_sum = total[conv_weight.shape[0] :].reshape(norm_stack.shape)
    input_grad = grad_mix + scatter_near(reorder(mul("kcn,kdc->nd", grad_qkv, w_qkv, BF), 0))
    qkv_grad = mul("nd,kcn->dkc", gathered_in, grad_qkv, BF)
    qkv_share = jnp.moveaxis(sum_at_owner(qkv_grad, share), 0, 1)
    return (
        output,
        input_grad,
        qkv_share,
        out_share,
        conv_grad,
        up_share,
        down_share,
        norm_sum[0],
        norm_sum[1],
        norm_sum[2],
        norm_sum[3],
    )


def solution(mesh):
    rows = P(("fsdp", "tensor"), None)
    cross = P("tensor", "fsdp")
    stacked = P(None, "fsdp", "tensor")
    return jax.shard_map(
        shards,
        mesh=mesh,
        in_specs=(rows, stacked, cross, P(), P("fsdp", "tensor"), cross, P(), P(), P(), P(), rows),
        out_specs=(rows, rows, stacked, cross, P(), P("fsdp", "tensor"), cross, P(), P(), P(), P()),
        check_vma=False,
    )
```

```python
import jax
import jax.numpy as jnp
from jax import lax
from jax.experimental import pallas as pl
from jax.experimental.pallas import tpu as pltpu
from jax.sharding import PartitionSpec as P
HD=64; LANDMARKS=64; ITERS=6
F32=jnp.float32; BF=jnp.bfloat16
SPAN=256; REACH=128

def dot(a,b,ca,cb):
    return lax.dot_general(a,b,(((ca,),(cb,)),((),())),preferred_element_type=F32)

def low(a):
    return a.astype(BF)

def parts(a):
    high=a.astype(BF)
    return high,(a-high.astype(F32)).astype(BF)

def dot3(a,b,ca,cb):
    ah,al=a if isinstance(a,tuple) else parts(a)
    bh,bl=b if isinstance(b,tuple) else parts(b)
    return dot(ah,bh,ca,cb)+(dot(ah,bl,ca,cb)+dot(al,bh,ca,cb))

def segments(length):
    row=lax.broadcasted_iota(jnp.int32,(LANDMARKS,length),0)
    col=lax.broadcasted_iota(jnp.int32,(LANDMARKS,length),1)
    size=length//LANDMARKS
    first=row*size
    return jnp.where((col>=first)&(col<first+size),1.0,0.0).astype(BF)

def soft_rows(s):
    e=jnp.exp(s-jnp.max(s,axis=1,keepdims=True))
    return e*(1.0/jnp.sum(e,axis=1,keepdims=True))

def soft_cols(s):
    e=jnp.exp(s-jnp.max(s,axis=0,keepdims=True))
    return e*(1.0/jnp.sum(e,axis=0,keepdims=True))

def marks_body(qkv_ref,marks_ref,k2_ref,peak_ref):
    heads=k2_ref.shape[0]
    length=qkv_ref.shape[2]
    seg=segments(length)
    factor=HD**-0.25
    scale=factor/(length//LANDMARKS)
    peak_ref[...]=jnp.zeros(peak_ref.shape,F32)
    for h in range(heads):
        rows=slice(h*HD,(h+1)*HD)
        found=[]
        for j in range(2):
            x=qkv_ref[j,rows,:]
            xh,xl=parts(x)
            m=(dot(seg,xh,1,1)+dot(seg,xl,1,1))*scale
            marks_ref[h,j]=m
            found.append(m)
        inner=dot3(found[0],found[1],1,1)
        k2=soft_rows(inner)
        k2_ref[h]=k2
        top=jnp.max(jnp.sum(k2,axis=0,keepdims=True),axis=1,keepdims=True)
        peak_ref[h:h+1,:]=jnp.broadcast_to(top,(1,128))

def band(taps_row):
    wide=jnp.broadcast_to(taps_row,(SPAN,taps_row.shape[1]))
    return pltpu.roll(wide,0,1,stride=1,stride_axis=0)

def windows(pad_ref,x,length):
    pad_ref[:,:REACH]=jnp.zeros((HD,REACH),BF)
    pad_ref[:,REACH+length:]=jnp.zeros((HD,REACH),BF)
    pad_ref[:,REACH:REACH+length]=low(x)
    return jnp.concatenate([pad_ref[:,b*SPAN:b*SPAN+SPAN+2*REACH] for b in range(length//SPAN)],axis=0)

def kernels_body(qkv_ref,marks_ref,taps_ref,k1_ref,k3_ref,sum_ref,conv_ref,pad_ref):
    length=qkv_ref.shape[2]
    factor=HD**-0.25
    ql=marks_ref[0,0]; kl=marks_ref[0,1]
    k1_ref[...]=soft_cols(dot3(kl,qkv_ref[0]*factor,1,0))
    k3=soft_rows(dot3(ql,qkv_ref[1]*factor,1,0))
    k3_ref[...]=k3
    v=qkv_ref[2]
    sum_ref[...]=dot(low(k3),low(v),1,1)
    wins=windows(pad_ref,v,length)
    out=dot(wins,low(band(taps_ref[0,0:1,:])),1,1)
    for b in range(length//SPAN):
        conv_ref[:,b*SPAN:(b+1)*SPAN]=out[b*HD:(b+1)*HD,:]

def eye():
    r=lax.broadcasted_iota(jnp.int32,(LANDMARKS,LANDMARKS),0)
    c=lax.broadcasted_iota(jnp.int32,(LANDMARKS,LANDMARKS),1)
    return jnp.where(r==c,1.0,0.0)

def mix_body(k2_ref,peak_ref,*refs):
    heads=k2_ref.shape[0]
    sums,k1s,convs=(refs[j*heads:(j+1)*heads] for j in range(3))
    ctx_ref,hist_ref,fin_ref=refs[3*heads:]
    ident=eye()
    k2=[k2_ref[h] for h in range(heads)]
    k2p=[parts(x) for x in k2]
    start=tuple(k2[h].T*(1.0/peak_ref[h:h+1,0:1]) for h in range(heads))
    def advance(step,a):
        ap=[parts(x) for x in a]
        p=[dot3(k2p[h],ap[h],1,0) for h in range(heads)]
        pp=[parts(x) for x in p]
        t=[15.0*ident-dot3(pp[h],7.0*ident-p[h],1,0) for h in range(heads)]
        u=[13.0*ident-dot3(pp[h],t[h],1,0) for h in range(heads)]
        for h in range(heads):
            hist_ref[h,step,0]=a[h]; hist_ref[h,step,1]=p[h]
            hist_ref[h,step,2]=t[h]; hist_ref[h,step,3]=u[h]
        return tuple(0.25*dot3(ap[h],u[h],1,0) for h in range(heads))
    a=lax.fori_loop(0,ITERS,advance,start)
    for h in range(heads):
        car=dot3(a[h],sums[h][...],1,0)
        fin_ref[h,0]=a[h]; fin_ref[h,1]=car
        rows=slice(h*HD,(h+1)*HD)
        ctx_ref[rows,:]=(dot(low(car),low(k1s[h][...]),0,0)+convs[h][...]).astype(BF)

def back_marks_body(g_ref,k2_ref,peak_ref,hist_ref,fin_ref,vwin_ref,*refs):
    heads=k2_ref.shape[0]
    k1s,sums=refs[:heads],refs[heads:2*heads]
    dsum_ref,dk2_ref,dinv_ref,dtap_ref,pad_ref,gst_ref=refs[2*heads:]
    length=g_ref.shape[1]
    ident=eye()
    dinv_ref[...]=jnp.zeros(dinv_ref.shape,F32)
    dtap_ref[...]=jnp.zeros(dtap_ref.shape,F32)
    k2p=[parts(k2_ref[h]) for h in range(heads)]
    da=[]
    for h in range(heads):
        rows=slice(h*HD,(h+1)*HD)
        dcar=dot(low(k1s[h][...]),g_ref[rows,:],1,1)
        dp_=parts(dcar)
        da.append(dot3(dp_,sums[h][...],1,1))
        dsum_ref[h]=dot3(fin_ref[h,0],dp_,0,0)
    zero=jnp.zeros((LANDMARKS,LANDMARKS),F32)
    def retreat(done,carry):
        step=ITERS-1-done
        da,dk2=carry
        nxt=[]; out=[]
        for h in range(heads):
            A=parts(hist_ref[h,step,0]); P=hist_ref[h,step,1]; T2=hist_ref[h,step,2]; T3=hist_ref[h,step,3]
            Pp=parts(P); D=parts(da[h])
            dT3=0.25*dot3(A,D,0,0)
            dAn=0.25*dot3(D,T3,1,1)
            d3=parts(dT3)
            dT2=-dot3(Pp,d3,0,0)
            d2=parts(dT2)
            dP=-dot3(d3,T2,1,1)-dot3(d2,7.0*ident-P,1,1)+dot3(Pp,d2,0,0)
            dPp=parts(dP)
            out.append(dk2[h]+dot3(dPp,A,1,1))
            nxt.append(dAn+dot3(k2p[h],dPp,0,0))
        return tuple(nxt),tuple(out)
    da,dk2=lax.fori_loop(0,ITERS,retreat,(tuple(da),(zero,)*heads))
    for h in range(heads):
        inv=1.0/peak_ref[h:h+1,0:1]
        dk2_ref[h]=dk2[h]+da[h].T*inv
        prod=da[h]*k2_ref[h].T
        tot=jnp.sum(jnp.sum(prod,axis=0,keepdims=True),axis=1,keepdims=True)
        dinv_ref[h:h+1,:]=jnp.broadcast_to(tot,(1,128))
    r=lax.broadcasted_iota(jnp.int32,(SPAN,SPAN),0)
    c=lax.broadcasted_iota(jnp.int32,(SPAN,SPAN),1)
    flip=jnp.where(r+c==SPAN-1,1.0,0.0).astype(BF)
    for h in range(heads):
        wins=windows(pad_ref,vwin_ref[0,h*HD:(h+1)*HD,:],length)
        for b in range(length//SPAN):
            gst_ref[b*HD:(b+1)*HD,:]=g_ref[h*HD:(h+1)*HD,b*SPAN:(b+1)*SPAN]
        m=dot(low(dot(gst_ref[...],flip,1,0)),wins,0,0)
        m=pltpu.roll(m,0,1,stride=1,stride_axis=0)
        s=jnp.sum(m,axis=0,keepdims=True)
        dtap_ref[h:h+1,:]=s

def back_body(qkv_ref,g_ref,marks_ref,k1_ref,k3_ref,sum_ref,fin_ref,dsum_ref,taps_ref,dqs_ref,dks_ref,dv_ref,dmarks_ref,pad_ref):
    length=qkv_ref.shape[2]
    factor=HD**-0.25
    g=g_ref[...]
    car=low(fin_ref[0,1]); dsum=dsum_ref[0]
    k1=k1_ref[...]
    dk1=dot(car,g,1,0)
    ds1=low(k1*(dk1-jnp.sum(k1*dk1,axis=0,keepdims=True)))
    dqs_ref[...]=dot(low(marks_ref[0,1]),ds1,0,0)
    dmarks_ref[1]=dot(ds1,low(qkv_ref[0]*factor),1,1)
    k3=k3_ref[...]
    v=qkv_ref[2]
    dl=low(dsum)
    delta=jnp.sum(dsum*sum_ref[...],axis=1,keepdims=True)
    ds3=low(k3*(dot(dl,low(v),1,0)-delta))
    dks_ref[...]=dot(low(marks_ref[0,0]),ds3,0,0)
    dmarks_ref[0]=dot(ds3,low(qkv_ref[1]*factor),1,1)
    wins=windows(pad_ref,g,length)
    out=dot(wins,low(band(taps_ref[0,1:2,:])),1,1)
    dv=dot(dl,low(k3),0,0)
    for b in range(length//SPAN):
        dv_ref[:,b*SPAN:(b+1)*SPAN]=(dv[:,b*SPAN:(b+1)*SPAN]+out[b*HD:(b+1)*HD,:]).astype(BF)

def close_body(k2_ref,dk2_ref,own_ref,marks_ref,*refs):
    heads=k2_ref.shape[0]
    dmarks,dqs,dks,dvs=(refs[j*heads:(j+1)*heads] for j in range(4))
    out_ref=refs[4*heads]
    length=out_ref.shape[1]
    width=heads*HD
    factor=HD**-0.25
    seg=segments(length)
    scale=factor/(length//LANDMARKS)
    for h in range(heads):
        k2=k2_ref[h]
        sums=jnp.sum(k2,axis=0,keepdims=True)
        hit=jnp.where(sums==jnp.max(sums,axis=1,keepdims=True),1.0,0.0)
        hit=hit*(1.0/jnp.sum(hit,axis=1,keepdims=True))
        dk2=dk2_ref[h]+hit*own_ref[h:h+1,0:1]
        ds2=k2*(dk2-jnp.sum(k2*dk2,axis=1,keepdims=True))
        dp=parts(ds2)
        dql=dmarks[h][0]+dot3(dp,marks_ref[h,1],1,0)
        dkl=dmarks[h][1]+dot3(dp,marks_ref[h,0],0,0)
        for j,(d,s_ref) in enumerate(((dql,dqs[h]),(dkl,dks[h]))):
            dh,dl=parts(d*scale)
            spread=dot(dh,seg,0,0)+dot(dl,seg,0,0)
            out_ref[j*width+h*HD:j*width+(h+1)*HD,:]=(s_ref[...]*factor+spread).astype(BF)
        out_ref[2*width+h*HD:2*width+(h+1)*HD,:]=dvs[h][...]

def tap_rows(conv):
    _,count=conv.shape
    width=SPAN+2*REACH
    left=REACH-count//2
    pad=((0,0),(left,width-left-count))
    return jnp.stack([jnp.pad(conv,pad),jnp.pad(conv[:,::-1],pad)],axis=1)

VM=pl.BlockSpec(memory_space=pltpu.VMEM)
def sds(shape,dt=F32): return jax.ShapeDtypeStruct(shape,dt)
LIM=56*2**20
def params(): return pltpu.CompilerParams(vmem_limit_bytes=LIM)

def marks_call(qkv,heads):
    n=qkv.shape[2]
    return pl.pallas_call(marks_body,out_shape=(sds((heads,2,LANDMARKS,HD)),sds((heads,LANDMARKS,LANDMARKS)),sds((8,128))),
        in_specs=[pl.BlockSpec((2,heads*HD,n),lambda i:(0,0,0))],grid=(1,),
        out_specs=(pl.BlockSpec((heads,2,LANDMARKS,HD),lambda i:(0,0,0,0)),pl.BlockSpec((heads,LANDMARKS,LANDMARKS),lambda i:(0,0,0)),pl.BlockSpec((8,128),lambda i:(0,0))),
        name="marks",compiler_params=params())(qkv)

def fixed(shape,*at):
    return pl.BlockSpec(shape,lambda i:at)

def full(a):
    return fixed(a.shape,*(0,)*len(a.shape))

def out_full(*shapes):
    return tuple(full(x) for x in shapes)

def kernels_call(qkv,marks,taps,h):
    n=qkv.shape[2]
    outs=(sds((HD,n)),sds((HD,n)),sds((LANDMARKS,HD)),sds((HD,n)))
    return pl.pallas_call(kernels_body,grid=(1,),
        in_specs=[fixed((3,HD,n),0,h,0),fixed((1,2,LANDMARKS,HD),h,0,0,0),fixed((1,2,taps.shape[2]),h,0,0)],
        out_specs=out_full(*outs),out_shape=outs,
        scratch_shapes=[pltpu.VMEM((HD,n+2*REACH),BF)],name="kernels",compiler_params=params())(qkv,marks,taps)

def mix_call(k2,peak,sums,k1s,convs,heads):
    n=k1s[0].shape[1]
    args=(k2,peak,*sums,*k1s,*convs)
    return pl.pallas_call(mix_body,in_specs=[VM]*len(args),out_specs=(VM,VM,VM),
        out_shape=(sds((heads*HD,n),BF),sds((heads,ITERS,4,LANDMARKS,LANDMARKS)),sds((heads,2,LANDMARKS,LANDMARKS))),
        name="mix",compiler_params=params())(*args)

def back_marks_call(g,k2,peak,hist,fin,qkv,k1s,sums,heads):
    n=g.shape[1]
    args=(g,k2,peak,hist,fin)
    outs=(sds((heads,LANDMARKS,HD)),sds((heads,LANDMARKS,LANDMARKS)),sds((8,128)),sds((8,SPAN+2*REACH)))
    return pl.pallas_call(back_marks_body,grid=(1,),
        in_specs=[full(a) for a in args]+[fixed((1,heads*HD,n),2,0,0)]+[full(a) for a in (*k1s,*sums)],
        out_specs=out_full(*outs),out_shape=outs,
        scratch_shapes=[pltpu.VMEM((HD,n+2*REACH),BF),pltpu.VMEM((n//SPAN*HD,SPAN),BF)],
        name="back_marks",compiler_params=params())(*args,qkv,*k1s,*sums)

def back_call(qkv,g,marks,k1,k3,summ,fin,dsum,taps,h):
    n=g.shape[1]
    outs=(sds((HD,n)),sds((HD,n)),sds((HD,n),BF),sds((2,LANDMARKS,HD)))
    return pl.pallas_call(back_body,grid=(1,),
        in_specs=[fixed((3,HD,n),0,h,0),fixed((HD,n),h,0),fixed((1,2,LANDMARKS,HD),h,0,0,0),full(k1),full(k3),full(summ),
            fixed((1,2,LANDMARKS,HD),h,0,0,0),fixed((1,LANDMARKS,HD),h,0,0),fixed((1,2,taps.shape[2]),h,0,0)],
        out_specs=out_full(*outs),out_shape=outs,
        scratch_shapes=[pltpu.VMEM((HD,n+2*REACH),BF)],name="back",compiler_params=params())(qkv,g,marks,k1,k3,summ,fin,dsum,taps)

def close_call(k2,dk2,own,marks,dmarks,dqs,dks,dvs,heads):
    n=dqs[0].shape[1]
    args=(k2,dk2,own,marks,*dmarks,*dqs,*dks,*dvs)
    return pl.pallas_call(close_body,in_specs=[VM]*len(args),out_specs=VM,out_shape=sds((3*heads*HD,n),BF),
        name="close",compiler_params=params())(*args)


def xor_pairs(size, bit):
    return [(i, i ^ bit) for i in range(size)]


def xor_swap(value, axis, bit):
    return lax.ppermute(value, axis, xor_pairs(lax.axis_size(axis), bit))


def power_of_two(size):
    return size & (size - 1) == 0


def everywhere(value, axis, combine, plain):
    size = lax.axis_size(axis)
    if not power_of_two(size):
        return plain(value, axis)
    bit = 1
    while bit < size:
        far = xor_swap(value, axis, bit)
        value = combine(value, far)
        bit *= 2
    return value


def sum_everywhere(value, axis):
    return everywhere(value, axis, jnp.add, lax.psum)


def gather_near(value):
    far = xor_swap(value, "tensor", 2)
    near = xor_swap(value, "tensor", 1)
    last = xor_swap(far, "tensor", 1)
    return jnp.concatenate([value, near, far, last], axis=0)


def scatter_near(value):
    rows = value.shape[0] // 4
    block = lambda j: value[j * rows : (j + 1) * rows]
    far = xor_swap(jnp.concatenate([block(3)], axis=0), "tensor", 1)
    near = xor_swap(block(1), "tensor", 1)
    sent = block(2).astype(F32) + far.astype(F32)
    got = xor_swap(sent.astype(BF), "tensor", 2)
    return block(0).astype(F32) + near.astype(F32) + got.astype(F32)


def gather_pair(value):
    return jnp.concatenate([value, xor_swap(value, "tensor", 1)], axis=0)


def product_scattered(spec, value, weight):
    half = value.shape[0] // 2
    far = xor_swap(mul(spec, value[half:], weight, BF), "tensor", 1)
    return mul(spec, value[:half], weight) + far.astype(F32)


def gather_rows(value):
    size = lax.axis_size("fsdp")
    if not power_of_two(size) or size > 8:
        return lax.all_gather(value, "fsdp", axis=0)
    place = lax.axis_index("fsdp")
    stack = jnp.stack([value if k == 0 else xor_swap(value, "fsdp", k) for k in range(size)])
    return jnp.concatenate(
        [lax.dynamic_slice_in_dim(stack, place ^ k, 1, 0) for k in range(size)], axis=0
    )


def reorder(value, axis):
    place = lax.axis_index("tensor")
    rows = value.shape[axis] // 4
    return jnp.concatenate(
        [lax.dynamic_slice_in_dim(value, (place ^ j) * rows, rows, axis) for j in range(4)], axis=axis
    )


def sum_at_owner(value, rows):
    count = lax.axis_size("fsdp")
    tiles = value.reshape(count, rows, *value.shape[1:])
    arrived = lax.all_to_all(tiles, "fsdp", split_axis=0, concat_axis=0, tiled=True)
    return arrived.astype(F32).sum(axis=0)


def gelu_both(value):
    scale = (2.0 / jnp.pi) ** 0.5
    square = value * value
    bent = jnp.tanh(value * (scale + (scale * 0.044715) * square))
    half = 0.5 + 0.5 * bent
    slope = half + (0.5 * value) * (1.0 - bent * bent) * (scale + (3.0 * 0.044715 * scale) * square)
    return value * half, slope


def norm_forward(rows, gain, shift):
    center = rows - jnp.mean(rows, axis=-1, keepdims=True)
    spread = jnp.mean(center * center, axis=-1, keepdims=True)
    factor = lax.rsqrt(spread + 1e-05)
    normed = center * factor
    return (normed * gain + shift, normed, factor)


def norm_backward(cotan, normed, factor, gain):
    scaled = cotan * gain
    return factor * (
        scaled
        - jnp.mean(scaled, axis=-1, keepdims=True)
        - normed * jnp.mean(scaled * normed, axis=-1, keepdims=True)
    )


def norm_params(cotan, normed):
    return (jnp.sum(cotan * normed, axis=0), jnp.sum(cotan, axis=0))


def mul(spec, a, b, kind=F32):
    return jnp.einsum(spec, a, b, preferred_element_type=F32).astype(kind)


def shards(
    inputs,
    qkv_weight,
    out_weight,
    conv_weight,
    up_weight,
    down_weight,
    mix_gain,
    mix_bias,
    feed_gain,
    feed_bias,
    out_grad,
):
    place = lax.axis_index("tensor")
    columns = qkv_weight.shape[2]
    heads = columns // HD
    units = up_weight.shape[1]
    share = qkv_weight.shape[1]
    gathered_in = reorder(gather_near(inputs.astype(BF)), 0)
    direct = jnp.concatenate([qkv_weight[0], qkv_weight[1], qkv_weight[2], out_weight.T], axis=1)
    direct = gather_rows(direct)
    direct = direct.reshape(-1, direct.shape[2])
    w_qkv = direct[:, : 3 * columns]
    w_out = direct[:, 3 * columns :]
    packed = jnp.concatenate([up_weight, down_weight.T], axis=1)
    packed_far = xor_swap(packed, "tensor", 2)
    packed = jnp.concatenate(
        [packed[:, :units], packed_far[:, :units], packed[:, units:], packed_far[:, units:]], axis=1
    )
    w_rest = lax.all_gather(packed, "fsdp", axis=0, tiled=True)
    w_up = w_rest[:, : 2 * units]
    w_down = w_rest[:, 2 * units :]
    qkv = mul("nd,dc->cn", gathered_in, w_qkv).reshape(3, columns, -1)
    conv_local = lax.dynamic_slice_in_dim(conv_weight, place * heads, heads, 0)
    taps = tap_rows(conv_local)
    marks, k2, peak_local = marks_call(qkv, heads)
    peak = everywhere(peak_local, "fsdp", jnp.maximum, lax.pmax)
    found = []
    for h in range(heads):
        found.append(kernels_call(qkv, marks, taps, h))
    k1, k3, summary, conv = zip(*found)
    context, hist, fin = mix_call(k2, peak, summary, k1, conv, heads)
    context_own = reorder(context, 1)
    attended = scatter_near(mul("cn,dc->nd", context_own, w_out, BF))
    mixed_rows, normed_mix, factor_mix = norm_forward(inputs + attended, mix_gain, mix_bias)
    mixed_low = gather_pair(mixed_rows.astype(BF))
    act, slope = gelu_both(mul("nd,df->nf", mixed_low, w_up))
    act, slope = act.astype(BF), slope.astype(BF)
    fed = product_scattered("nf,df->nd", act, w_down)
    output, normed_feed, factor_feed = norm_forward(mixed_rows + fed, feed_gain, feed_bias)
    grad_feed = norm_backward(out_grad, normed_feed, factor_feed, feed_gain)
    feed_gain_part, feed_bias_part = norm_params(out_grad, normed_feed)
    grad_down = gather_pair(grad_feed.astype(BF))
    grad_up = (mul("nd,df->nf", grad_down, w_down) * slope.astype(F32)).astype(BF)
    grad_mixed_rows = grad_feed + product_scattered("nf,df->nd", grad_up, w_up)
    down_pair = mul("nd,nf->df", grad_down, act, BF)
    down_pair = sum_at_owner(down_pair, share)
    far = xor_swap(down_pair[:, units:].astype(BF), "tensor", 2)
    down_share = (down_pair[:, :units] + far.astype(F32)).T
    grad_mix = norm_backward(grad_mixed_rows, normed_mix, factor_mix, mix_gain)
    mix_gain_part, mix_bias_part = norm_params(grad_mixed_rows, normed_mix)
    grad_attended = gather_near(grad_mix.astype(BF))
    far = mul("nd,nf->df", mixed_low, grad_up[:, units:], BF)
    far = xor_swap(far, "tensor", 2)
    up_sum = mul("nd,nf->df", mixed_low, grad_up[:, :units]) + far.astype(F32)
    up_share = sum_at_owner(up_sum.astype(BF), share)
    out_grad_part = mul("nd,cn->dc", grad_attended, context_own, BF)
    grad_context = reorder(mul("nd,dc->cn", grad_attended, w_out, BF), 1)
    dsum, dk2, dinv, dtap = back_marks_call(grad_context, k2, peak, hist, fin, qkv, k1, summary, heads)
    first = SPAN - 1 + REACH - conv_weight.shape[1] // 2
    dtap = dtap[:, first : first + 128]
    norm_stack = jnp.stack([mix_gain_part, mix_bias_part, feed_gain_part, feed_bias_part])
    norm_rows = norm_stack.reshape(-1, 128)
    total = sum_everywhere(jnp.concatenate([dinv, dtap, norm_rows], axis=0), "fsdp")
    own = jnp.where(peak_local == peak, -total[:8] / (peak * peak), 0.0)
    found = []
    for h in range(heads):
        found.append(
            back_call(qkv, grad_context, marks, k1[h], k3[h], summary[h], fin, dsum, taps, h)
        )
    dqs, dks, dv, dmarks = zip(*found)
    grad_qkv = close_call(k2, dk2, own, marks, dmarks, dqs, dks, dv, heads)
    conv_full = lax.dynamic_update_slice_in_dim(
        jnp.zeros((conv_weight.shape[0], 128), F32), total[8 : 8 + heads], place * heads, 0
    )
    total = sum_everywhere(jnp.concatenate([conv_full, total[16:]], axis=0), "tensor")
    conv_grad = total[: conv_weight.shape[0], : conv_weight.shape[1]]
    norm_sum = total[conv_weight.shape[0] :].reshape(norm_stack.shape)
    qkv_grad = mul("nd,cn->dc", gathered_in, grad_qkv, BF)
    qkv_share = sum_at_owner(jnp.concatenate([qkv_grad, out_grad_part], axis=1), share)
    out_share = qkv_share[:, 3 * columns :].T
    qkv_share = jnp.moveaxis(qkv_share[:, : 3 * columns].reshape(share, 3, columns), 1, 0)
    input_part = reorder(mul("cn,dc->nd", grad_qkv, w_qkv, BF), 0)
    input_grad = grad_mix + scatter_near(input_part)
    return (
        output,
        input_grad,
        qkv_share,
        out_share,
        conv_grad,
        up_share,
        down_share,
        norm_sum[0],
        norm_sum[1],
        norm_sum[2],
        norm_sum[3],
    )


def solution(mesh):
    rows = P(("fsdp", "tensor"), None)
    cross = P("tensor", "fsdp")
    stacked = P(None, "fsdp", "tensor")

    return jax.shard_map(
        shards,
        mesh=mesh,
        in_specs=(rows, stacked, cross, P(), P("fsdp", "tensor"), cross, P(), P(), P(), P(), rows),
        out_specs=(rows, rows, stacked, cross, P(), P("fsdp", "tensor"), cross, P(), P(), P(), P()),
        check_vma=False,
    )
```

```python
import jax
import jax.numpy as jnp
from jax import lax
from jax.experimental import pallas as pl
from jax.experimental.pallas import tpu as pltpu
from jax.sharding import PartitionSpec as P
HD=64; LANDMARKS=64; ITERS=6
F32=jnp.float32; BF=jnp.bfloat16
SPAN=256; REACH=128

def dot(a,b,ca,cb):
    return lax.dot_general(a,b,(((ca,),(cb,)),((),())),preferred_element_type=F32)

def low(a):
    return a.astype(BF)

def parts(a):
    high=a.astype(BF)
    return high,(a-high.astype(F32)).astype(BF)

def dot3(a,b,ca,cb):
    ah,al=a if isinstance(a,tuple) else parts(a)
    bh,bl=b if isinstance(b,tuple) else parts(b)
    return dot(ah,bh,ca,cb)+(dot(ah,bl,ca,cb)+dot(al,bh,ca,cb))

def segments(length):
    row=lax.broadcasted_iota(jnp.int32,(LANDMARKS,length),0)
    col=lax.broadcasted_iota(jnp.int32,(LANDMARKS,length),1)
    size=length//LANDMARKS
    first=row*size
    return jnp.where((col>=first)&(col<first+size),1.0,0.0).astype(BF)

def soft_rows(s):
    e=jnp.exp(s-jnp.max(s,axis=1,keepdims=True))
    return e*(1.0/jnp.sum(e,axis=1,keepdims=True))

def soft_cols(s):
    e=jnp.exp(s-jnp.max(s,axis=0,keepdims=True))
    return e*(1.0/jnp.sum(e,axis=0,keepdims=True))

def marks_body(qkv_ref,marks_ref,k2_ref,peak_ref):
    heads=k2_ref.shape[0]
    length=qkv_ref.shape[2]
    seg=segments(length)
    factor=HD**-0.25
    scale=factor/(length//LANDMARKS)
    peak_ref[...]=jnp.zeros(peak_ref.shape,F32)
    x=qkv_ref[...].reshape(2*heads*HD,length)
    xh,xl=parts(x)
    every=(dot(xh,seg,1,1)+dot(xl,seg,1,1))*scale
    for h in range(heads):
        found=[]
        for j in range(2):
            at=(j*heads+h)*HD
            m=every[at:at+HD,:].T
            marks_ref[h,j]=m
            found.append(m)
        inner=dot3(found[0],found[1],1,1)
        k2=soft_rows(inner)
        k2_ref[h]=k2
        top=jnp.max(jnp.sum(k2,axis=0,keepdims=True),axis=1,keepdims=True)
        peak_ref[h:h+1,:]=jnp.broadcast_to(top,(1,128))

def band(taps_row):
    wide=jnp.broadcast_to(taps_row,(SPAN,taps_row.shape[1]))
    return pltpu.roll(wide,0,1,stride=1,stride_axis=0)

def windows(pad_ref,x,length):
    pad_ref[:,:REACH]=jnp.zeros((HD,REACH),BF)
    pad_ref[:,REACH+length:]=jnp.zeros((HD,REACH),BF)
    pad_ref[:,REACH:REACH+length]=low(x)
    return jnp.concatenate([pad_ref[:,b*SPAN:b*SPAN+SPAN+2*REACH] for b in range(length//SPAN)],axis=0)

def kernels_body(qkv_ref,marks_ref,taps_ref,k1_ref,k3_ref,sum_ref,conv_ref,pad_ref):
    length=qkv_ref.shape[2]
    factor=HD**-0.25
    ql=marks_ref[0,0]; kl=marks_ref[0,1]
    k1_ref[...]=soft_cols(dot3(kl,qkv_ref[0]*factor,1,0))
    k3=soft_rows(dot3(ql,qkv_ref[1]*factor,1,0))
    k3_ref[...]=k3
    v=qkv_ref[2]
    sum_ref[...]=dot(low(k3),low(v),1,1)
    wins=windows(pad_ref,v,length)
    out=dot(wins,low(band(taps_ref[0,0:1,:])),1,1)
    for b in range(length//SPAN):
        conv_ref[:,b*SPAN:(b+1)*SPAN]=out[b*HD:(b+1)*HD,:]

def eye():
    r=lax.broadcasted_iota(jnp.int32,(LANDMARKS,LANDMARKS),0)
    c=lax.broadcasted_iota(jnp.int32,(LANDMARKS,LANDMARKS),1)
    return jnp.where(r==c,1.0,0.0)

def mix_body(k2_ref,peak_ref,*refs):
    heads=k2_ref.shape[0]
    sums,k1s,convs=(refs[j*heads:(j+1)*heads] for j in range(3))
    ctx_ref,hist_ref,fin_ref=refs[3*heads:]
    ident=eye()
    k2=[k2_ref[h] for h in range(heads)]
    k2p=[parts(x) for x in k2]
    start=tuple(k2[h].T*(1.0/peak_ref[h:h+1,0:1]) for h in range(heads))
    def advance(step,a):
        ap=[parts(x) for x in a]
        p=[dot3(k2p[h],ap[h],1,0) for h in range(heads)]
        pp=[parts(x) for x in p]
        t=[15.0*ident-dot3(pp[h],7.0*ident-p[h],1,0) for h in range(heads)]
        u=[13.0*ident-dot3(pp[h],t[h],1,0) for h in range(heads)]
        for h in range(heads):
            hist_ref[h,step,0]=a[h]; hist_ref[h,step,1]=p[h]
            hist_ref[h,step,2]=t[h]; hist_ref[h,step,3]=u[h]
        return tuple(0.25*dot3(ap[h],u[h],1,0) for h in range(heads))
    a=lax.fori_loop(0,ITERS,advance,start)
    for h in range(heads):
        car=dot3(a[h],sums[h][...],1,0)
        fin_ref[h,0]=a[h]; fin_ref[h,1]=car
        rows=slice(h*HD,(h+1)*HD)
        ctx_ref[rows,:]=(dot(low(car),low(k1s[h][...]),0,0)+convs[h][...]).astype(BF)

def back_marks_body(g_ref,k2_ref,peak_ref,hist_ref,fin_ref,vwin_ref,*refs):
    heads=k2_ref.shape[0]
    k1s,sums=refs[:heads],refs[heads:2*heads]
    dsum_ref,dk2_ref,dinv_ref,dtap_ref,pad_ref,gst_ref=refs[2*heads:]
    length=g_ref.shape[1]
    ident=eye()
    dinv_ref[...]=jnp.zeros(dinv_ref.shape,F32)
    dtap_ref[...]=jnp.zeros(dtap_ref.shape,F32)
    k2p=[parts(k2_ref[h]) for h in range(heads)]
    da=[]
    for h in range(heads):
        rows=slice(h*HD,(h+1)*HD)
        dcar=dot(low(k1s[h][...]),g_ref[rows,:],1,1)
        dp_=parts(dcar)
        da.append(dot3(dp_,sums[h][...],1,1))
        dsum_ref[h]=dot3(fin_ref[h,0],dp_,0,0)
    zero=jnp.zeros((LANDMARKS,LANDMARKS),F32)
    def retreat(done,carry):
        step=ITERS-1-done
        da,dk2=carry
        nxt=[]; out=[]
        for h in range(heads):
            A=parts(hist_ref[h,step,0]); P=hist_ref[h,step,1]; T2=hist_ref[h,step,2]; T3=hist_ref[h,step,3]
            Pp=parts(P); D=parts(da[h])
            dT3=0.25*dot3(A,D,0,0)
            dAn=0.25*dot3(D,T3,1,1)
            d3=parts(dT3)
            dT2=-dot3(Pp,d3,0,0)
            d2=parts(dT2)
            dP=-dot3(d3,T2,1,1)-dot3(d2,7.0*ident-P,1,1)+dot3(Pp,d2,0,0)
            dPp=parts(dP)
            out.append(dk2[h]+dot3(dPp,A,1,1))
            nxt.append(dAn+dot3(k2p[h],dPp,0,0))
        return tuple(nxt),tuple(out)
    da,dk2=lax.fori_loop(0,ITERS,retreat,(tuple(da),(zero,)*heads))
    for h in range(heads):
        inv=1.0/peak_ref[h:h+1,0:1]
        dk2_ref[h]=dk2[h]+da[h].T*inv
        prod=da[h]*k2_ref[h].T
        tot=jnp.sum(jnp.sum(prod,axis=0,keepdims=True),axis=1,keepdims=True)
        dinv_ref[h:h+1,:]=jnp.broadcast_to(tot,(1,128))
    r=lax.broadcasted_iota(jnp.int32,(SPAN,SPAN),0)
    c=lax.broadcasted_iota(jnp.int32,(SPAN,SPAN),1)
    flip=jnp.where(r+c==SPAN-1,1.0,0.0).astype(BF)
    for h in range(heads):
        wins=windows(pad_ref,vwin_ref[0,h*HD:(h+1)*HD,:],length)
        for b in range(length//SPAN):
            gst_ref[b*HD:(b+1)*HD,:]=g_ref[h*HD:(h+1)*HD,b*SPAN:(b+1)*SPAN]
        m=dot(low(dot(gst_ref[...],flip,1,0)),wins,0,0)
        m=pltpu.roll(m,0,1,stride=1,stride_axis=0)
        s=jnp.sum(m,axis=0,keepdims=True)
        dtap_ref[h:h+1,:]=s

def back_body(qkv_ref,g_ref,marks_ref,k1_ref,k3_ref,sum_ref,fin_ref,dsum_ref,taps_ref,dqs_ref,dks_ref,dv_ref,dmarks_ref,pad_ref):
    length=qkv_ref.shape[2]
    factor=HD**-0.25
    g=g_ref[...]
    car=low(fin_ref[0,1]); dsum=dsum_ref[0]
    k1=k1_ref[...]
    dk1=dot(car,g,1,0)
    ds1=low(k1*(dk1-jnp.sum(k1*dk1,axis=0,keepdims=True)))
    dqs_ref[...]=dot(low(marks_ref[0,1]),ds1,0,0)
    dmarks_ref[1]=dot(ds1,low(qkv_ref[0]*factor),1,1)
    k3=k3_ref[...]
    v=qkv_ref[2]
    dl=low(dsum)
    delta=jnp.sum(dsum*sum_ref[...],axis=1,keepdims=True)
    ds3=low(k3*(dot(dl,low(v),1,0)-delta))
    dks_ref[...]=dot(low(marks_ref[0,0]),ds3,0,0)
    dmarks_ref[0]=dot(ds3,low(qkv_ref[1]*factor),1,1)
    wins=windows(pad_ref,g,length)
    out=dot(wins,low(band(taps_ref[0,1:2,:])),1,1)
    dv=dot(dl,low(k3),0,0)
    for b in range(length//SPAN):
        dv_ref[:,b*SPAN:(b+1)*SPAN]=(dv[:,b*SPAN:(b+1)*SPAN]+out[b*HD:(b+1)*HD,:]).astype(BF)

def close_body(k2_ref,dk2_ref,own_ref,marks_ref,*refs):
    heads=k2_ref.shape[0]
    dmarks,dqs,dks,dvs=(refs[j*heads:(j+1)*heads] for j in range(4))
    out_ref=refs[4*heads]
    length=out_ref.shape[1]
    width=heads*HD
    factor=HD**-0.25
    seg=segments(length)
    scale=factor/(length//LANDMARKS)
    grads=[[None]*heads for _ in range(2)]
    for h in range(heads):
        k2=k2_ref[h]
        sums=jnp.sum(k2,axis=0,keepdims=True)
        hit=jnp.where(sums==jnp.max(sums,axis=1,keepdims=True),1.0,0.0)
        hit=hit*(1.0/jnp.sum(hit,axis=1,keepdims=True))
        dk2=dk2_ref[h]+hit*own_ref[h:h+1,0:1]
        ds2=k2*(dk2-jnp.sum(k2*dk2,axis=1,keepdims=True))
        dp=parts(ds2)
        grads[0][h]=((dmarks[h][0]+dot3(dp,marks_ref[h,1],1,0))*scale).T
        grads[1][h]=((dmarks[h][1]+dot3(dp,marks_ref[h,0],0,0))*scale).T
    dh,dl=parts(jnp.concatenate(grads[0]+grads[1],axis=0))
    spread=dot(dh,seg,1,0)+dot(dl,seg,1,0)
    for j,parts_of in enumerate((dqs,dks)):
        for h in range(heads):
            rows=slice(j*width+h*HD,j*width+(h+1)*HD)
            out_ref[rows,:]=(parts_of[h][...]*factor+spread[rows,:]).astype(BF)
    for h in range(heads):
        out_ref[2*width+h*HD:2*width+(h+1)*HD,:]=dvs[h][...]

def tap_rows(conv):
    _,count=conv.shape
    width=SPAN+2*REACH
    left=REACH-count//2
    pad=((0,0),(left,width-left-count))
    return jnp.stack([jnp.pad(conv,pad),jnp.pad(conv[:,::-1],pad)],axis=1)

VM=pl.BlockSpec(memory_space=pltpu.VMEM)
def sds(shape,dt=F32): return jax.ShapeDtypeStruct(shape,dt)
LIM=24*2**20
def params(): return pltpu.CompilerParams(vmem_limit_bytes=LIM)

def marks_call(qkv,heads):
    n=qkv.shape[2]
    return pl.pallas_call(marks_body,out_shape=(sds((heads,2,LANDMARKS,HD)),sds((heads,LANDMARKS,LANDMARKS)),sds((8,128))),
        in_specs=[pl.BlockSpec((2,heads*HD,n),lambda i:(0,0,0))],grid=(1,),
        out_specs=(pl.BlockSpec((heads,2,LANDMARKS,HD),lambda i:(0,0,0,0)),pl.BlockSpec((heads,LANDMARKS,LANDMARKS),lambda i:(0,0,0)),pl.BlockSpec((8,128),lambda i:(0,0))),
        name="marks",compiler_params=params())(qkv)

def fixed(shape,*at):
    return pl.BlockSpec(shape,lambda i:at)

def full(a):
    return fixed(a.shape,*(0,)*len(a.shape))

def out_full(*shapes):
    return tuple(full(x) for x in shapes)

def kernels_call(qkv,marks,taps,h):
    n=qkv.shape[2]
    outs=(sds((HD,n)),sds((HD,n)),sds((LANDMARKS,HD)),sds((HD,n)))
    return pl.pallas_call(kernels_body,grid=(1,),
        in_specs=[fixed((3,HD,n),0,h,0),fixed((1,2,LANDMARKS,HD),h,0,0,0),fixed((1,2,taps.shape[2]),h,0,0)],
        out_specs=out_full(*outs),out_shape=outs,
        scratch_shapes=[pltpu.VMEM((HD,n+2*REACH),BF)],name="kernels",compiler_params=params())(qkv,marks,taps)

def mix_call(k2,peak,sums,k1s,convs,heads):
    n=k1s[0].shape[1]
    args=(k2,peak,*sums,*k1s,*convs)
    return pl.pallas_call(mix_body,in_specs=[VM]*len(args),out_specs=(VM,VM,VM),
        out_shape=(sds((heads*HD,n),BF),sds((heads,ITERS,4,LANDMARKS,LANDMARKS)),sds((heads,2,LANDMARKS,LANDMARKS))),
        name="mix",compiler_params=params())(*args)

def back_marks_call(g,k2,peak,hist,fin,qkv,k1s,sums,heads):
    n=g.shape[1]
    args=(g,k2,peak,hist,fin)
    outs=(sds((heads,LANDMARKS,HD)),sds((heads,LANDMARKS,LANDMARKS)),sds((8,128)),sds((8,SPAN+2*REACH)))
    return pl.pallas_call(back_marks_body,grid=(1,),
        in_specs=[full(a) for a in args]+[fixed((1,heads*HD,n),2,0,0)]+[full(a) for a in (*k1s,*sums)],
        out_specs=out_full(*outs),out_shape=outs,
        scratch_shapes=[pltpu.VMEM((HD,n+2*REACH),BF),pltpu.VMEM((n//SPAN*HD,SPAN),BF)],
        name="back_marks",compiler_params=params())(*args,qkv,*k1s,*sums)

def back_call(qkv,g,marks,k1,k3,summ,fin,dsum,taps,h):
    n=g.shape[1]
    outs=(sds((HD,n)),sds((HD,n)),sds((HD,n),BF),sds((2,LANDMARKS,HD)))
    return pl.pallas_call(back_body,grid=(1,),
        in_specs=[fixed((3,HD,n),0,h,0),fixed((HD,n),h,0),fixed((1,2,LANDMARKS,HD),h,0,0,0),full(k1),full(k3),full(summ),
            fixed((1,2,LANDMARKS,HD),h,0,0,0),fixed((1,LANDMARKS,HD),h,0,0),fixed((1,2,taps.shape[2]),h,0,0)],
        out_specs=out_full(*outs),out_shape=outs,
        scratch_shapes=[pltpu.VMEM((HD,n+2*REACH),BF)],name="back",compiler_params=params())(qkv,g,marks,k1,k3,summ,fin,dsum,taps)

def close_call(k2,dk2,own,marks,dmarks,dqs,dks,dvs,heads):
    n=dqs[0].shape[1]
    args=(k2,dk2,own,marks,*dmarks,*dqs,*dks,*dvs)
    return pl.pallas_call(close_body,in_specs=[VM]*len(args),out_specs=VM,out_shape=sds((3*heads*HD,n),BF),
        name="close",compiler_params=params())(*args)


def xor_pairs(size, bit):
    return [(i, i ^ bit) for i in range(size)]


def xor_swap(value, axis, bit):
    return lax.ppermute(value, axis, xor_pairs(lax.axis_size(axis), bit))


def power_of_two(size):
    return size & (size - 1) == 0


def everywhere(value, axis, combine, plain):
    size = lax.axis_size(axis)
    if not power_of_two(size):
        return plain(value, axis)
    bit = 1
    while bit < size:
        far = xor_swap(value, axis, bit)
        value = combine(value, far)
        bit *= 2
    return value


def sum_everywhere(value, axis):
    return everywhere(value, axis, jnp.add, lax.psum)


def gather_near(value):
    far = xor_swap(value, "tensor", 2)
    near = xor_swap(value, "tensor", 1)
    last = xor_swap(far, "tensor", 1)
    return jnp.concatenate([value, near, far, last], axis=0)


def scatter_near(value):
    rows = value.shape[0] // 4
    block = lambda j: value[j * rows : (j + 1) * rows]
    far = xor_swap(jnp.concatenate([block(3)], axis=0), "tensor", 1)
    near = xor_swap(block(1), "tensor", 1)
    sent = block(2).astype(F32) + far.astype(F32)
    got = xor_swap(sent.astype(BF), "tensor", 2)
    return block(0).astype(F32) + near.astype(F32) + got.astype(F32)


def gather_pair(value):
    return jnp.concatenate([value, xor_swap(value, "tensor", 1)], axis=0)


def product_scattered(spec, value, weight):
    half = value.shape[0] // 2
    far = xor_swap(mul(spec, value[half:], weight, BF), "tensor", 1)
    return mul(spec, value[:half], weight) + far.astype(F32)


def gather_rows(value):
    size = lax.axis_size("fsdp")
    if not power_of_two(size) or size > 8:
        return lax.all_gather(value, "fsdp", axis=0)
    place = lax.axis_index("fsdp")
    stack = jnp.stack([value if k == 0 else xor_swap(value, "fsdp", k) for k in range(size)])
    return jnp.concatenate(
        [lax.dynamic_slice_in_dim(stack, place ^ k, 1, 0) for k in range(size)], axis=0
    )


def reorder(value, axis):
    place = lax.axis_index("tensor")
    rows = value.shape[axis] // 4
    return jnp.concatenate(
        [lax.dynamic_slice_in_dim(value, (place ^ j) * rows, rows, axis) for j in range(4)], axis=axis
    )


def sum_at_owner(value, rows):
    count = lax.axis_size("fsdp")
    tiles = value.reshape(count, rows, *value.shape[1:])
    arrived = lax.all_to_all(tiles, "fsdp", split_axis=0, concat_axis=0, tiled=True)
    return arrived.astype(F32).sum(axis=0)


def gelu_both(value):
    scale = (2.0 / jnp.pi) ** 0.5
    square = value * value
    bent = jnp.tanh(value * (scale + (scale * 0.044715) * square))
    half = 0.5 + 0.5 * bent
    slope = half + (0.5 * value) * (1.0 - bent * bent) * (scale + (3.0 * 0.044715 * scale) * square)
    return value * half, slope


def norm_forward(rows, gain, shift):
    center = rows - jnp.mean(rows, axis=-1, keepdims=True)
    spread = jnp.mean(center * center, axis=-1, keepdims=True)
    factor = lax.rsqrt(spread + 1e-05)
    normed = center * factor
    return (normed * gain + shift, normed, factor)


def norm_backward(cotan, normed, factor, gain):
    scaled = cotan * gain
    return factor * (
        scaled
        - jnp.mean(scaled, axis=-1, keepdims=True)
        - normed * jnp.mean(scaled * normed, axis=-1, keepdims=True)
    )


def norm_params(cotan, normed):
    return (jnp.sum(cotan * normed, axis=0), jnp.sum(cotan, axis=0))


def mul(spec, a, b, kind=F32):
    return jnp.einsum(spec, a, b, preferred_element_type=F32).astype(kind)


def shards(
    inputs,
    qkv_weight,
    out_weight,
    conv_weight,
    up_weight,
    down_weight,
    mix_gain,
    mix_bias,
    feed_gain,
    feed_bias,
    out_grad,
):
    place = lax.axis_index("tensor")
    columns = qkv_weight.shape[2]
    heads = columns // HD
    units = up_weight.shape[1]
    share = qkv_weight.shape[1]
    gathered_in = reorder(gather_near(inputs.astype(BF)), 0)
    direct = jnp.concatenate([qkv_weight[0], qkv_weight[1], qkv_weight[2], out_weight.T], axis=1)
    direct = gather_rows(direct)
    direct = direct.reshape(-1, direct.shape[2])
    w_qkv = direct[:, : 3 * columns]
    w_out = direct[:, 3 * columns :]
    packed = jnp.concatenate([up_weight, down_weight.T], axis=1)
    packed_far = xor_swap(packed, "tensor", 2)
    packed = jnp.concatenate(
        [packed[:, :units], packed_far[:, :units], packed[:, units:], packed_far[:, units:]], axis=1
    )
    packed, direct = lax.optimization_barrier((packed, direct))
    w_rest = lax.all_gather(packed, "fsdp", axis=0, tiled=True)
    w_up = w_rest[:, : 2 * units]
    w_down = w_rest[:, 2 * units :]
    qkv = mul("nd,dc->cn", gathered_in, w_qkv).reshape(3, columns, -1)
    conv_local = lax.dynamic_slice_in_dim(conv_weight, place * heads, heads, 0)
    taps = tap_rows(conv_local)
    marks, k2, peak_local = marks_call(qkv, heads)
    peak = everywhere(peak_local, "fsdp", jnp.maximum, lax.pmax)
    found = []
    for h in range(heads):
        found.append(kernels_call(qkv, marks, taps, h))
    k1, k3, summary, conv = zip(*found)
    context, hist, fin = mix_call(k2, peak, summary, k1, conv, heads)
    context_own = reorder(context, 1)
    attended = scatter_near(mul("cn,dc->nd", context_own, w_out, BF))
    mixed_rows, normed_mix, factor_mix = norm_forward(inputs + attended, mix_gain, mix_bias)
    mixed_low = gather_pair(mixed_rows.astype(BF))
    act, slope = gelu_both(mul("nd,df->nf", mixed_low, w_up))
    act, slope = act.astype(BF), slope.astype(BF)
    fed = product_scattered("nf,df->nd", act, w_down)
    output, normed_feed, factor_feed = norm_forward(mixed_rows + fed, feed_gain, feed_bias)
    grad_feed = norm_backward(out_grad, normed_feed, factor_feed, feed_gain)
    feed_gain_part, feed_bias_part = norm_params(out_grad, normed_feed)
    grad_down = gather_pair(grad_feed.astype(BF))
    grad_up = (mul("nd,df->nf", grad_down, w_down) * slope.astype(F32)).astype(BF)
    grad_mixed_rows = grad_feed + product_scattered("nf,df->nd", grad_up, w_up)
    down_pair = mul("nd,nf->df", grad_down, act, BF)
    down_pair = sum_at_owner(down_pair, share)
    far = xor_swap(down_pair[:, units:].astype(BF), "tensor", 2)
    down_share = (down_pair[:, :units] + far.astype(F32)).T
    grad_mix = norm_backward(grad_mixed_rows, normed_mix, factor_mix, mix_gain)
    mix_gain_part, mix_bias_part = norm_params(grad_mixed_rows, normed_mix)
    grad_attended = gather_near(grad_mix.astype(BF))
    far = mul("nd,nf->df", mixed_low, grad_up[:, units:], BF)
    far = xor_swap(far, "tensor", 2)
    up_sum = mul("nd,nf->df", mixed_low, grad_up[:, :units]) + far.astype(F32)
    out_sum = mul("nd,cn->dc", grad_attended, context_own, BF)
    up_share = sum_at_owner(jnp.concatenate([up_sum.astype(BF), out_sum], axis=1), share)
    out_share = up_share[:, units:].T
    up_share = up_share[:, :units]
    grad_context = reorder(mul("nd,dc->cn", grad_attended, w_out, BF), 1)
    dsum, dk2, dinv, dtap = back_marks_call(grad_context, k2, peak, hist, fin, qkv, k1, summary, heads)
    first = SPAN - 1 + REACH - conv_weight.shape[1] // 2
    dtap = dtap[:, first : first + 128]
    norm_stack = jnp.stack([mix_gain_part, mix_bias_part, feed_gain_part, feed_bias_part])
    norm_rows = norm_stack.reshape(-1, 128)
    total = sum_everywhere(jnp.concatenate([dinv, dtap, norm_rows], axis=0), "fsdp")
    own = jnp.where(peak_local == peak, -total[:8] / (peak * peak), 0.0)
    found = []
    for h in range(heads):
        found.append(
            back_call(qkv, grad_context, marks, k1[h], k3[h], summary[h], fin, dsum, taps, h)
        )
    dqs, dks, dv, dmarks = zip(*found)
    grad_qkv = close_call(k2, dk2, own, marks, dmarks, dqs, dks, dv, heads)
    conv_full = lax.dynamic_update_slice_in_dim(
        jnp.zeros((conv_weight.shape[0], 128), F32), total[8 : 8 + heads], place * heads, 0
    )
    total = sum_everywhere(jnp.concatenate([conv_full, total[16:]], axis=0), "tensor")
    conv_grad = total[: conv_weight.shape[0], : conv_weight.shape[1]]
    norm_sum = total[conv_weight.shape[0] :].reshape(norm_stack.shape)
    qkv_grad = mul("nd,cn->dc", gathered_in, grad_qkv, BF)
    qkv_share = sum_at_owner(qkv_grad, share)
    qkv_share = jnp.moveaxis(qkv_share.reshape(share, 3, columns), 1, 0)
    input_part = reorder(mul("cn,dc->nd", grad_qkv, w_qkv, BF), 0)
    input_grad = grad_mix + scatter_near(input_part)
    return (
        output,
        input_grad,
        qkv_share,
        out_share,
        conv_grad,
        up_share,
        down_share,
        norm_sum[0],
        norm_sum[1],
        norm_sum[2],
        norm_sum[3],
    )


def solution(mesh):
    rows = P(("fsdp", "tensor"), None)
    cross = P("tensor", "fsdp")
    stacked = P(None, "fsdp", "tensor")

    return jax.shard_map(
        shards,
        mesh=mesh,
        in_specs=(rows, stacked, cross, P(), P("fsdp", "tensor"), cross, P(), P(), P(), P(), rows),
        out_specs=(rows, rows, stacked, cross, P(), P("fsdp", "tensor"), cross, P(), P(), P(), P()),
        check_vma=False,
    )
```

```python
import jax
import jax.numpy as jnp
from jax import lax
from jax.experimental import pallas as pl
from jax.experimental.pallas import tpu as pltpu
from jax.sharding import PartitionSpec as P
HD=64; LANDMARKS=64; ITERS=6
F32=jnp.float32; BF=jnp.bfloat16
SPAN=256; REACH=128

def dot(a,b,ca,cb):
    return lax.dot_general(a,b,(((ca,),(cb,)),((),())),preferred_element_type=F32)

def low(a):
    return a.astype(BF)

def parts(a):
    high=a.astype(BF)
    return high,(a-high.astype(F32)).astype(BF)

def dot3(a,b,ca,cb):
    ah,al=a if isinstance(a,tuple) else parts(a)
    bh,bl=b if isinstance(b,tuple) else parts(b)
    return dot(ah,bh,ca,cb)+(dot(ah,bl,ca,cb)+dot(al,bh,ca,cb))

def segments(length):
    row=lax.broadcasted_iota(jnp.int32,(LANDMARKS,length),0)
    col=lax.broadcasted_iota(jnp.int32,(LANDMARKS,length),1)
    size=length//LANDMARKS
    first=row*size
    return jnp.where((col>=first)&(col<first+size),1.0,0.0).astype(BF)

def soft_rows(s):
    e=jnp.exp(s-jnp.max(s,axis=1,keepdims=True))
    return e*(1.0/jnp.sum(e,axis=1,keepdims=True))

def soft_cols(s):
    e=jnp.exp(s-jnp.max(s,axis=0,keepdims=True))
    return e*(1.0/jnp.sum(e,axis=0,keepdims=True))

def marks_body(qkv_ref,marks_ref,k2_ref,peak_ref):
    heads=k2_ref.shape[0]
    length=qkv_ref.shape[2]
    seg=segments(length)
    factor=HD**-0.25
    scale=factor/(length//LANDMARKS)
    peak_ref[...]=jnp.zeros(peak_ref.shape,F32)
    x=qkv_ref[...].reshape(2*heads*HD,length)
    xh,xl=parts(x)
    every=(dot(xh,seg,1,1)+dot(xl,seg,1,1))*scale
    for h in range(heads):
        found=[]
        for j in range(2):
            at=(j*heads+h)*HD
            m=every[at:at+HD,:].T
            marks_ref[h,j]=m
            found.append(m)
        inner=dot3(found[0],found[1],1,1)
        k2=soft_rows(inner)
        k2_ref[h]=k2
        top=jnp.max(jnp.sum(k2,axis=0,keepdims=True),axis=1,keepdims=True)
        peak_ref[h:h+1,:]=jnp.broadcast_to(top,(1,128))

def band(taps_row):
    wide=jnp.broadcast_to(taps_row,(SPAN,taps_row.shape[1]))
    return pltpu.roll(wide,0,1,stride=1,stride_axis=0)

def windows(pad_ref,x,length):
    pad_ref[:,:REACH]=jnp.zeros((HD,REACH),BF)
    pad_ref[:,REACH+length:]=jnp.zeros((HD,REACH),BF)
    pad_ref[:,REACH:REACH+length]=low(x)
    return jnp.concatenate([pad_ref[:,b*SPAN:b*SPAN+SPAN+2*REACH] for b in range(length//SPAN)],axis=0)

def kernels_body(qkv_ref,marks_ref,taps_ref,save_ref,sum_ref,conv_ref,pad_ref):
    length=qkv_ref.shape[2]
    factor=HD**-0.25
    ql=marks_ref[0,0]; kl=marks_ref[0,1]
    qs=parts(qkv_ref[0]*factor)
    save_ref[0,0]=low(soft_cols(dot3(kl,qs,1,0)))
    ks=parts(qkv_ref[1]*factor)
    k3=low(soft_rows(dot3(ql,ks,1,0)))
    v=low(qkv_ref[2])
    save_ref[0,1]=k3; save_ref[0,2]=qs[0]; save_ref[0,3]=ks[0]; save_ref[0,4]=v
    sum_ref[0]=dot(k3,v,1,1)
    wins=windows(pad_ref,v,length)
    out=dot(wins,low(band(taps_ref[0,0:1,:])),1,1)
    for b in range(length//SPAN):
        conv_ref[:,b*SPAN:(b+1)*SPAN]=low(out[b*HD:(b+1)*HD,:])

def eye():
    r=lax.broadcasted_iota(jnp.int32,(LANDMARKS,LANDMARKS),0)
    c=lax.broadcasted_iota(jnp.int32,(LANDMARKS,LANDMARKS),1)
    return jnp.where(r==c,1.0,0.0)

def mix_body(k2_ref,peak_ref,sum_ref,k1_ref,conv_ref,ctx_ref,hist_ref,fin_ref):
    heads=k2_ref.shape[0]
    ident=eye()
    k2=[k2_ref[h] for h in range(heads)]
    k2p=[parts(x) for x in k2]
    start=tuple(k2[h].T*(1.0/peak_ref[h:h+1,0:1]) for h in range(heads))
    def advance(step,a):
        ap=[parts(x) for x in a]
        p=[dot3(k2p[h],ap[h],1,0) for h in range(heads)]
        pp=[parts(x) for x in p]
        t=[15.0*ident-dot3(pp[h],7.0*ident-p[h],1,0) for h in range(heads)]
        u=[13.0*ident-dot3(pp[h],t[h],1,0) for h in range(heads)]
        for h in range(heads):
            hist_ref[h,step,0]=a[h]; hist_ref[h,step,1]=p[h]
            hist_ref[h,step,2]=t[h]; hist_ref[h,step,3]=u[h]
        return tuple(0.25*dot3(ap[h],u[h],1,0) for h in range(heads))
    a=lax.fori_loop(0,ITERS,advance,start)
    for h in range(heads):
        car=dot3(a[h],sum_ref[h],1,0)
        fin_ref[h,0]=a[h]; fin_ref[h,1]=car
        rows=slice(h*HD,(h+1)*HD)
        ctx_ref[rows,:]=(dot(low(car),k1_ref[h,0],0,0)+conv_ref[rows,:].astype(F32)).astype(BF)

def back_marks_body(g_ref,k2_ref,peak_ref,hist_ref,fin_ref,k1_ref,sum_ref,v_ref,dsum_ref,dk2_ref,dinv_ref,dtap_ref,pad_ref,gst_ref):
    heads=k2_ref.shape[0]
    length=g_ref.shape[1]
    ident=eye()
    dinv_ref[...]=jnp.zeros(dinv_ref.shape,F32)
    dtap_ref[...]=jnp.zeros(dtap_ref.shape,F32)
    k2p=[parts(k2_ref[h]) for h in range(heads)]
    da=[]
    for h in range(heads):
        rows=slice(h*HD,(h+1)*HD)
        dcar=dot(k1_ref[h,0],g_ref[rows,:],1,1)
        dp_=parts(dcar)
        da.append(dot3(dp_,sum_ref[h],1,1))
        dsum_ref[h]=dot3(fin_ref[h,0],dp_,0,0)
    zero=jnp.zeros((LANDMARKS,LANDMARKS),F32)
    def retreat(done,carry):
        step=ITERS-1-done
        da,dk2=carry
        nxt=[]; out=[]
        for h in range(heads):
            A=parts(hist_ref[h,step,0]); P=hist_ref[h,step,1]; T2=hist_ref[h,step,2]; T3=hist_ref[h,step,3]
            Pp=parts(P); D=parts(da[h])
            dT3=0.25*dot3(A,D,0,0)
            dAn=0.25*dot3(D,T3,1,1)
            d3=parts(dT3)
            dT2=-dot3(Pp,d3,0,0)
            d2=parts(dT2)
            dP=-dot3(d3,T2,1,1)-dot3(d2,7.0*ident-P,1,1)+dot3(Pp,d2,0,0)
            dPp=parts(dP)
            out.append(dk2[h]+dot3(dPp,A,1,1))
            nxt.append(dAn+dot3(k2p[h],dPp,0,0))
        return tuple(nxt),tuple(out)
    da,dk2=lax.fori_loop(0,ITERS,retreat,(tuple(da),(zero,)*heads))
    for h in range(heads):
        inv=1.0/peak_ref[h:h+1,0:1]
        dk2_ref[h]=dk2[h]+da[h].T*inv
        prod=da[h]*k2_ref[h].T
        tot=jnp.sum(jnp.sum(prod,axis=0,keepdims=True),axis=1,keepdims=True)
        dinv_ref[h:h+1,:]=jnp.broadcast_to(tot,(1,128))
    r=lax.broadcasted_iota(jnp.int32,(SPAN,SPAN),0)
    c=lax.broadcasted_iota(jnp.int32,(SPAN,SPAN),1)
    flip=jnp.where(r+c==SPAN-1,1.0,0.0).astype(BF)
    for h in range(heads):
        wins=windows(pad_ref,v_ref[h,0],length)
        for b in range(length//SPAN):
            gst_ref[b*HD:(b+1)*HD,:]=g_ref[h*HD:(h+1)*HD,b*SPAN:(b+1)*SPAN]
        m=dot(low(dot(gst_ref[...],flip,1,0)),wins,0,0)
        m=pltpu.roll(m,0,1,stride=1,stride_axis=0)
        s=jnp.sum(m,axis=0,keepdims=True)
        dtap_ref[h:h+1,:]=s

def back_body(save_ref,g_ref,marks_ref,sum_ref,fin_ref,dsum_ref,taps_ref,dqkv_ref,dmarks_ref,pad_ref):
    length=g_ref.shape[1]
    g=g_ref[...]
    car=low(fin_ref[0,1]); dsum=dsum_ref[0]
    k1=save_ref[0,0].astype(F32)
    dk1=dot(car,g,1,0)
    ds1=low(k1*(dk1-jnp.sum(k1*dk1,axis=0,keepdims=True)))
    dqkv_ref[0]=low(dot(low(marks_ref[0,1]),ds1,0,0))
    dmarks_ref[0,1]=dot(ds1,save_ref[0,2],1,1)
    k3=save_ref[0,1]
    dl=low(dsum)
    delta=jnp.sum(dsum*sum_ref[0],axis=1,keepdims=True)
    ds3=low(k3.astype(F32)*(dot(dl,save_ref[0,4],1,0)-delta))
    dqkv_ref[1]=low(dot(low(marks_ref[0,0]),ds3,0,0))
    dmarks_ref[0,0]=dot(ds3,save_ref[0,3],1,1)
    wins=windows(pad_ref,g,length)
    out=dot(wins,low(band(taps_ref[0,1:2,:])),1,1)
    dv=dot(dl,k3,0,0)
    for b in range(length//SPAN):
        dqkv_ref[2,:,b*SPAN:(b+1)*SPAN]=(dv[:,b*SPAN:(b+1)*SPAN]+out[b*HD:(b+1)*HD,:]).astype(BF)

def close_body(k2_ref,dk2_ref,own_ref,marks_ref,dmarks_ref,dqkv_ref,out_ref):
    heads=k2_ref.shape[0]
    length=out_ref.shape[1]
    width=heads*HD
    factor=HD**-0.25
    seg=segments(length)
    scale=factor/(length//LANDMARKS)
    grads=[[None]*heads for _ in range(2)]
    for h in range(heads):
        k2=k2_ref[h]
        sums=jnp.sum(k2,axis=0,keepdims=True)
        hit=jnp.where(sums==jnp.max(sums,axis=1,keepdims=True),1.0,0.0)
        hit=hit*(1.0/jnp.sum(hit,axis=1,keepdims=True))
        dk2=dk2_ref[h]+hit*own_ref[h:h+1,0:1]
        ds2=k2*(dk2-jnp.sum(k2*dk2,axis=1,keepdims=True))
        dp=parts(ds2)
        grads[0][h]=((dmarks_ref[h,0]+dot3(dp,marks_ref[h,1],1,0))*scale).T
        grads[1][h]=((dmarks_ref[h,1]+dot3(dp,marks_ref[h,0],0,0))*scale).T
    dh,dl=parts(jnp.concatenate(grads[0]+grads[1],axis=0))
    spread=dot(dh,seg,1,0)+dot(dl,seg,1,0)
    for j in range(2):
        rows=slice(j*width,(j+1)*width)
        out_ref[rows,:]=(dqkv_ref[j].astype(F32)*factor+spread[rows,:]).astype(BF)
    out_ref[2*width:,:]=dqkv_ref[2]

def tap_rows(conv):
    _,count=conv.shape
    width=SPAN+2*REACH
    left=REACH-count//2
    pad=((0,0),(left,width-left-count))
    return jnp.stack([jnp.pad(conv,pad),jnp.pad(conv[:,::-1],pad)],axis=1)

VM=pl.BlockSpec(memory_space=pltpu.VMEM)
def sds(shape,dt=F32): return jax.ShapeDtypeStruct(shape,dt)
LIM=12*2**20
def params(): return pltpu.CompilerParams(vmem_limit_bytes=LIM)

def marks_call(qkv,heads):
    n=qkv.shape[2]
    return pl.pallas_call(marks_body,out_shape=(sds((heads,2,LANDMARKS,HD)),sds((heads,LANDMARKS,LANDMARKS)),sds((8,128))),
        in_specs=[pl.BlockSpec((2,heads*HD,n),lambda i:(0,0,0))],grid=(1,),
        out_specs=(pl.BlockSpec((heads,2,LANDMARKS,HD),lambda i:(0,0,0,0)),pl.BlockSpec((heads,LANDMARKS,LANDMARKS),lambda i:(0,0,0)),pl.BlockSpec((8,128),lambda i:(0,0))),
        name="marks",compiler_params=params())(qkv)

def fixed(shape,*at):
    return pl.BlockSpec(shape,lambda i:at)

def full(a):
    return fixed(a.shape,*(0,)*len(a.shape))

def out_full(*shapes):
    return tuple(full(x) for x in shapes)

def each(shape,spot):
    return pl.BlockSpec(shape,lambda h:tuple(h if d==spot else 0 for d in range(len(shape))))

def kernels_call(qkv,marks,taps,heads):
    n=qkv.shape[2]
    return pl.pallas_call(kernels_body,grid=(heads,),
        in_specs=[each((3,HD,n),1),each((1,2,LANDMARKS,HD),0),each((1,2,taps.shape[2]),0)],
        out_specs=(each((1,5,HD,n),0),each((1,LANDMARKS,HD),0),each((HD,n),0)),
        out_shape=(sds((heads,5,HD,n),BF),sds((heads,LANDMARKS,HD)),sds((heads*HD,n),BF)),
        scratch_shapes=[pltpu.VMEM((HD,n+2*REACH),BF)],name="kernels",compiler_params=params())(qkv,marks,taps)

def mix_call(k2,peak,sums,save,conv,heads):
    n=save.shape[3]
    outs=(sds((heads*HD,n),BF),sds((heads,ITERS,4,LANDMARKS,LANDMARKS)),sds((heads,2,LANDMARKS,LANDMARKS)))
    return pl.pallas_call(mix_body,grid=(1,),
        in_specs=[full(k2),full(peak),full(sums),fixed((heads,1,HD,n),0,0,0,0),full(conv)],
        out_specs=out_full(*outs),out_shape=outs,name="mix",compiler_params=params())(k2,peak,sums,save,conv)

def back_marks_call(g,k2,peak,hist,fin,save,sums,heads):
    n=g.shape[1]
    args=(g,k2,peak,hist,fin)
    outs=(sds((heads,LANDMARKS,HD)),sds((heads,LANDMARKS,LANDMARKS)),sds((8,128)),sds((8,SPAN+2*REACH)))
    return pl.pallas_call(back_marks_body,grid=(1,),
        in_specs=[full(a) for a in args]+[fixed((heads,1,HD,n),0,0,0,0),full(sums),fixed((heads,1,HD,n),0,4,0,0)],
        out_specs=out_full(*outs),out_shape=outs,
        scratch_shapes=[pltpu.VMEM((HD,n+2*REACH),BF),pltpu.VMEM((n//SPAN*HD,SPAN),BF)],
        name="back_marks",compiler_params=params())(*args,save,sums,save)

def back_call(save,g,marks,sums,fin,dsum,taps,heads):
    n=g.shape[1]
    sq=lambda: each((1,LANDMARKS,HD),0)
    two=lambda: each((1,2,LANDMARKS,HD),0)
    return pl.pallas_call(back_body,grid=(heads,),
        in_specs=[each((1,5,HD,n),0),each((HD,n),0),two(),sq(),two(),sq(),each((1,2,taps.shape[2]),0)],
        out_specs=(each((3,HD,n),1),two()),
        out_shape=(sds((3,heads*HD,n),BF),sds((heads,2,LANDMARKS,HD))),
        scratch_shapes=[pltpu.VMEM((HD,n+2*REACH),BF)],name="back",compiler_params=params())(save,g,marks,sums,fin,dsum,taps)

def close_call(k2,dk2,own,marks,dmarks,dqkv):
    n=dqkv.shape[2]
    return pl.pallas_call(close_body,in_specs=[VM]*6,out_specs=VM,out_shape=sds((dqkv.shape[0]*dqkv.shape[1],n),BF),
        name="close",compiler_params=params())(k2,dk2,own,marks,dmarks,dqkv)

def final_body(grad_ref,own_ref,near_ref,far_ref,out_ref):
    out_ref[...]=grad_ref[...]+own_ref[...].astype(F32)+near_ref[...].astype(F32)+far_ref[...].astype(F32)

def final_call(grad,own,near,far):
    rows,width=grad.shape
    step=rows//4
    block=pl.BlockSpec((step,width),lambda i:(i,0))
    return pl.pallas_call(final_body,grid=(4,),in_specs=[block]*4,out_specs=block,out_shape=sds(grad.shape),
        name="final",compiler_params=params())(grad,own,near,far)


def xor_pairs(size, bit):
    return [(i, i ^ bit) for i in range(size)]


def xor_swap(value, axis, bit):
    return lax.ppermute(value, axis, xor_pairs(lax.axis_size(axis), bit))


def power_of_two(size):
    return size & (size - 1) == 0


def everywhere(value, axis, combine, plain):
    size = lax.axis_size(axis)
    if not power_of_two(size):
        return plain(value, axis)
    bit = 1
    while bit < size:
        far = xor_swap(value, axis, bit)
        value = combine(value, far)
        bit *= 2
    return value


def sum_everywhere(value, axis):
    return everywhere(value, axis, jnp.add, lax.psum)


def gather_near(value):
    far = xor_swap(value, "tensor", 2)
    near = xor_swap(value, "tensor", 1)
    last = xor_swap(far, "tensor", 1)
    return jnp.concatenate([value, near, far, last], axis=0)


def scatter_near(value):
    rows = value.shape[0] // 4
    block = lambda j: value[j * rows : (j + 1) * rows]
    last = xor_swap(block(3), "tensor", 1)
    sent = (block(2).astype(F32) + last.astype(F32)).astype(BF)
    far = xor_swap(sent, "tensor", 2)
    near = xor_swap(block(1), "tensor", 1)
    return block(0), near, far


def gather_pair(value):
    return jnp.concatenate([value, xor_swap(value, "tensor", 1)], axis=0)


def product_scattered(spec, value, weight):
    half = value.shape[0] // 2
    far = xor_swap(mul(spec, value[half:], weight, BF), "tensor", 1)
    return mul(spec, value[:half], weight) + far.astype(F32)


def gather_rows(value):
    size = lax.axis_size("fsdp")
    if size != 8:
        return lax.all_gather(value, "fsdp", axis=0)
    place = lax.axis_index("fsdp")
    width = value.shape[1] // 2
    left, right = value[:, :width], value[:, width:]
    right = jnp.stack([right, xor_swap(right, "fsdp", 1)])
    left = jnp.stack([left] + [xor_swap(left, "fsdp", k) for k in (2, 4, 6)])
    right = jnp.stack([right] + [xor_swap(right, "fsdp", k) for k in (2, 4, 6)])
    left = jnp.stack([left, xor_swap(left, "fsdp", 1)], axis=1)

    def ordered(both):
        flat = both.reshape(size, *both.shape[2:])
        return jnp.concatenate(
            [lax.dynamic_slice_in_dim(flat, place ^ k, 1, 0) for k in range(size)], axis=0
        )

    return jnp.concatenate([ordered(left), ordered(right)], axis=2)


def reorder(value, axis):
    place = lax.axis_index("tensor")
    rows = value.shape[axis] // 4
    return jnp.concatenate(
        [lax.dynamic_slice_in_dim(value, (place ^ j) * rows, rows, axis) for j in range(4)], axis=axis
    )


def sum_at_owner(values, rows):
    count = lax.axis_size("fsdp")
    if count % 2:
        tiles = jnp.concatenate(values, axis=1).reshape(count, rows, -1)
        arrived = lax.all_to_all(tiles, "fsdp", split_axis=0, concat_axis=0, tiled=True)
        return arrived.astype(F32).sum(axis=0)
    side = lax.axis_index("fsdp") % 2
    pairs = []
    for value in values:
        tiles = value.reshape(count // 2, 2, rows, value.shape[1])
        sent = lax.dynamic_index_in_dim(tiles, 1 - side, 1, keepdims=False)
        got = xor_swap(sent, "fsdp", 1)
        kept = lax.dynamic_index_in_dim(tiles, side, 1, keepdims=False)
        pairs.append((kept.astype(F32) + got.astype(F32)).astype(BF))
    groups = [list(range(at, count, 2)) for at in range(2)]
    pair = pairs[0] if len(pairs) == 1 else jnp.concatenate(pairs, axis=2)
    arrived = lax.all_to_all(
        pair, "fsdp", split_axis=0, concat_axis=0, tiled=True, axis_index_groups=groups
    )
    return arrived.astype(F32).sum(axis=0)


def gelu_both(value):
    scale = (2.0 / jnp.pi) ** 0.5
    square = value * value
    bent = jnp.tanh(value * (scale + (scale * 0.044715) * square))
    half = 0.5 + 0.5 * bent
    slope = half + (0.5 * value) * (1.0 - bent * bent) * (scale + (3.0 * 0.044715 * scale) * square)
    return value * half, slope


def norm_forward(rows, gain, shift):
    center = rows - jnp.mean(rows, axis=-1, keepdims=True)
    spread = jnp.mean(center * center, axis=-1, keepdims=True)
    factor = lax.rsqrt(spread + 1e-05)
    normed = center * factor
    return (normed * gain + shift, normed, factor)


def norm_backward(cotan, normed, factor, gain):
    scaled = cotan * gain
    return factor * (
        scaled
        - jnp.mean(scaled, axis=-1, keepdims=True)
        - normed * jnp.mean(scaled * normed, axis=-1, keepdims=True)
    )


def norm_params(cotan, normed):
    return (jnp.sum(cotan * normed, axis=0), jnp.sum(cotan, axis=0))


def mul(spec, a, b, kind=F32):
    return jnp.einsum(spec, a, b, preferred_element_type=F32).astype(kind)


def shards(
    inputs,
    qkv_weight,
    out_weight,
    conv_weight,
    up_weight,
    down_weight,
    mix_gain,
    mix_bias,
    feed_gain,
    feed_bias,
    out_grad,
):
    place = lax.axis_index("tensor")
    columns = qkv_weight.shape[2]
    heads = columns // HD
    units = up_weight.shape[1]
    share = qkv_weight.shape[1]
    gathered_in = reorder(gather_near(inputs.astype(BF)), 0)
    direct = jnp.concatenate([qkv_weight[0], qkv_weight[1], qkv_weight[2], out_weight.T], axis=1)
    direct = gather_rows(direct)
    direct = direct.reshape(-1, direct.shape[2])
    w_qkv = direct[:, : 3 * columns]
    w_out = direct[:, 3 * columns :]
    packed = jnp.concatenate([up_weight, down_weight.T], axis=1)
    members = lax.axis_size("fsdp")
    groups = [[f * 4 + y * 2 + c for y in range(2) for f in range(members)] for c in range(2)]
    w_rest = lax.all_gather(packed, ("fsdp", "tensor"), axis=0, axis_index_groups=groups)
    w_rest = w_rest.reshape(2, -1, 2 * units)
    w_up = jnp.concatenate([w_rest[0, :, :units], w_rest[1, :, :units]], axis=1)
    w_down = jnp.concatenate([w_rest[0, :, units:], w_rest[1, :, units:]], axis=1)
    half = place // 2
    own_units = lambda value: lax.dynamic_slice_in_dim(value, half * units, units, 1)
    far_units = lambda value: lax.dynamic_slice_in_dim(value, (1 - half) * units, units, 1)
    qkv = mul("nd,dc->cn", gathered_in, w_qkv).reshape(3, columns, -1)
    conv_local = lax.dynamic_slice_in_dim(conv_weight, place * heads, heads, 0)
    taps = tap_rows(conv_local)
    marks, k2, peak_local = marks_call(qkv, heads)
    peak = everywhere(peak_local, "fsdp", jnp.maximum, lax.pmax)
    save, summary, conv = kernels_call(qkv, marks, taps, heads)
    context, hist, fin = mix_call(k2, peak, summary, save, conv, heads)
    context_own = reorder(context, 1)
    own, near, far = scatter_near(mul("cn,dc->nd", context_own, w_out, BF))
    attended = own.astype(F32) + near.astype(F32) + far.astype(F32)
    mixed_rows, normed_mix, factor_mix = norm_forward(inputs + attended, mix_gain, mix_bias)
    mixed_low = gather_pair(mixed_rows.astype(BF))
    act, slope = gelu_both(mul("nd,df->nf", mixed_low, w_up))
    act, slope = act.astype(BF), slope.astype(BF)
    fed = product_scattered("nf,df->nd", act, w_down)
    output, normed_feed, factor_feed = norm_forward(mixed_rows + fed, feed_gain, feed_bias)
    grad_feed = norm_backward(out_grad, normed_feed, factor_feed, feed_gain)
    feed_gain_part, feed_bias_part = norm_params(out_grad, normed_feed)
    grad_down = gather_pair(grad_feed.astype(BF))
    grad_up = (mul("nd,df->nf", grad_down, w_down) * slope.astype(F32)).astype(BF)
    grad_mixed_rows = grad_feed + product_scattered("nf,df->nd", grad_up, w_up)
    down_pair = mul("nd,nf->df", grad_down, act, BF)
    down_pair = sum_at_owner([down_pair], share)
    far = xor_swap(far_units(down_pair).astype(BF), "tensor", 2)
    down_share = (own_units(down_pair) + far.astype(F32)).T
    grad_mix = norm_backward(grad_mixed_rows, normed_mix, factor_mix, mix_gain)
    mix_gain_part, mix_bias_part = norm_params(grad_mixed_rows, normed_mix)
    grad_attended = gather_near(grad_mix.astype(BF))
    far = mul("nd,nf->df", mixed_low, far_units(grad_up), BF)
    far = xor_swap(far, "tensor", 2)
    up_sum = mul("nd,nf->df", mixed_low, own_units(grad_up)) + far.astype(F32)
    out_sum = mul("nd,cn->dc", grad_attended, context_own, BF)
    up_share = sum_at_owner([up_sum.astype(BF), out_sum], share)
    out_share = up_share[:, units:].T
    up_share = up_share[:, :units]
    grad_context = reorder(mul("nd,dc->cn", grad_attended, w_out, BF), 1)
    dsum, dk2, dinv, dtap = back_marks_call(grad_context, k2, peak, hist, fin, save, summary, heads)
    first = SPAN - 1 + REACH - conv_weight.shape[1] // 2
    dtap = dtap[:, first : first + 128]
    norm_stack = jnp.stack([mix_gain_part, mix_bias_part, feed_gain_part, feed_bias_part])
    norm_rows = norm_stack.reshape(-1, 128)
    total = sum_everywhere(jnp.concatenate([dinv, dtap, norm_rows], axis=0), "fsdp")
    own = jnp.where(peak_local == peak, -total[:8] / (peak * peak), 0.0)
    dqkv, dmarks = back_call(save, grad_context, marks, summary, fin, dsum, taps, heads)
    grad_qkv = close_call(k2, dk2, own, marks, dmarks, dqkv)
    conv_full = lax.dynamic_update_slice_in_dim(
        jnp.zeros((conv_weight.shape[0], 128), F32), total[8 : 8 + heads], place * heads, 0
    )
    total = sum_everywhere(jnp.concatenate([conv_full, total[16:]], axis=0), "tensor")
    conv_grad = total[: conv_weight.shape[0], : conv_weight.shape[1]]
    norm_sum = total[conv_weight.shape[0] :].reshape(norm_stack.shape)
    qkv_grad = mul("nd,cn->dc", gathered_in, grad_qkv, BF)
    qkv_share = sum_at_owner([qkv_grad], share)
    qkv_share = jnp.moveaxis(qkv_share.reshape(share, 3, columns), 1, 0)
    input_part = reorder(mul("cn,dc->nd", grad_qkv, w_qkv, BF), 0)
    input_grad = final_call(grad_mix, *scatter_near(input_part))
    return (
        output,
        input_grad,
        qkv_share,
        out_share,
        conv_grad,
        up_share,
        down_share,
        norm_sum[0],
        norm_sum[1],
        norm_sum[2],
        norm_sum[3],
    )


def solution(mesh):
    rows = P(("fsdp", "tensor"), None)
    cross = P("tensor", "fsdp")
    stacked = P(None, "fsdp", "tensor")

    return jax.shard_map(
        shards,
        mesh=mesh,
        in_specs=(rows, stacked, cross, P(), P("fsdp", "tensor"), cross, P(), P(), P(), P(), rows),
        out_specs=(rows, rows, stacked, cross, P(), P("fsdp", "tensor"), cross, P(), P(), P(), P()),
        check_vma=False,
    )
```

```python
import jax
import jax.numpy as jnp
from jax import lax
from jax.experimental import pallas as pl
from jax.experimental.pallas import tpu as pltpu
from jax.sharding import PartitionSpec as P
HD=64; LANDMARKS=64; ITERS=6
F32=jnp.float32; BF=jnp.bfloat16
SPAN=256; REACH=128

def dot(a,b,ca,cb):
    return lax.dot_general(a,b,(((ca,),(cb,)),((),())),preferred_element_type=F32)

def low(a):
    return a.astype(BF)

def parts(a):
    high=a.astype(BF)
    return high,(a-high.astype(F32)).astype(BF)

def dot3(a,b,ca,cb):
    ah,al=a if isinstance(a,tuple) else parts(a)
    bh,bl=b if isinstance(b,tuple) else parts(b)
    return dot(ah,bh,ca,cb)+(dot(ah,bl,ca,cb)+dot(al,bh,ca,cb))

def segments(length):
    row=lax.broadcasted_iota(jnp.int32,(LANDMARKS,length),0)
    col=lax.broadcasted_iota(jnp.int32,(LANDMARKS,length),1)
    size=length//LANDMARKS
    first=row*size
    return jnp.where((col>=first)&(col<first+size),1.0,0.0).astype(BF)

def soft_rows(s):
    e=jnp.exp(s-jnp.max(s,axis=1,keepdims=True))
    return e*(1.0/jnp.sum(e,axis=1,keepdims=True))

def soft_cols(s):
    e=jnp.exp(s-jnp.max(s,axis=0,keepdims=True))
    return e*(1.0/jnp.sum(e,axis=0,keepdims=True))

def marks_body(qkv_ref,marks_ref,k2_ref,peak_ref):
    heads=k2_ref.shape[0]
    length=qkv_ref.shape[2]
    seg=segments(length)
    factor=HD**-0.25
    scale=factor/(length//LANDMARKS)
    peak_ref[...]=jnp.zeros(peak_ref.shape,F32)
    x=qkv_ref[...].reshape(2*heads*HD,length)
    xh,xl=parts(x)
    every=(dot(xh,seg,1,1)+dot(xl,seg,1,1))*scale
    for h in range(heads):
        found=[]
        for j in range(2):
            at=(j*heads+h)*HD
            m=every[at:at+HD,:].T
            marks_ref[h,j]=m
            found.append(m)
        inner=dot3(found[0],found[1],1,1)
        k2=soft_rows(inner)
        k2_ref[h]=k2
        top=jnp.max(jnp.sum(k2,axis=0,keepdims=True),axis=1,keepdims=True)
        peak_ref[h:h+1,:]=jnp.broadcast_to(top,(1,128))

def band(taps_row):
    wide=jnp.broadcast_to(taps_row,(SPAN,taps_row.shape[1]))
    return pltpu.roll(wide,0,1,stride=1,stride_axis=0)

def windows(pad_ref,x,length):
    pad_ref[:,:REACH]=jnp.zeros((HD,REACH),BF)
    pad_ref[:,REACH+length:]=jnp.zeros((HD,REACH),BF)
    pad_ref[:,REACH:REACH+length]=low(x)
    return jnp.concatenate([pad_ref[:,b*SPAN:b*SPAN+SPAN+2*REACH] for b in range(length//SPAN)],axis=0)

def kernels_body(qkv_ref,marks_ref,taps_ref,save_ref,sum_ref,conv_ref,pad_ref):
    length=qkv_ref.shape[2]
    factor=HD**-0.25
    ql=marks_ref[0,0]; kl=marks_ref[0,1]
    qs=parts(qkv_ref[0]*factor)
    save_ref[0,0]=low(soft_cols(dot3(kl,qs,1,0)))
    ks=parts(qkv_ref[1]*factor)
    k3=low(soft_rows(dot3(ql,ks,1,0)))
    v=low(qkv_ref[2])
    save_ref[0,1]=k3; save_ref[0,2]=qs[0]; save_ref[0,3]=ks[0]; save_ref[0,4]=v
    sum_ref[0]=dot(k3,v,1,1)
    wins=windows(pad_ref,v,length)
    out=dot(wins,low(band(taps_ref[0,0:1,:])),1,1)
    for b in range(length//SPAN):
        conv_ref[:,b*SPAN:(b+1)*SPAN]=low(out[b*HD:(b+1)*HD,:])

def eye():
    r=lax.broadcasted_iota(jnp.int32,(LANDMARKS,LANDMARKS),0)
    c=lax.broadcasted_iota(jnp.int32,(LANDMARKS,LANDMARKS),1)
    return jnp.where(r==c,1.0,0.0)

def mix_body(k2_ref,peak_ref,sum_ref,k1_ref,conv_ref,ctx_ref,hist_ref,fin_ref):
    heads=k2_ref.shape[0]
    ident=eye()
    k2=[k2_ref[h] for h in range(heads)]
    k2p=[parts(x) for x in k2]
    start=tuple(k2[h].T*(1.0/peak_ref[h:h+1,0:1]) for h in range(heads))
    def advance(step,a):
        ap=[parts(x) for x in a]
        p=[dot3(k2p[h],ap[h],1,0) for h in range(heads)]
        pp=[parts(x) for x in p]
        t=[15.0*ident-dot3(pp[h],7.0*ident-p[h],1,0) for h in range(heads)]
        u=[13.0*ident-dot3(pp[h],t[h],1,0) for h in range(heads)]
        for h in range(heads):
            hist_ref[h,step,0]=a[h]; hist_ref[h,step,1]=p[h]
            hist_ref[h,step,2]=t[h]; hist_ref[h,step,3]=u[h]
        return tuple(0.25*dot3(ap[h],u[h],1,0) for h in range(heads))
    a=lax.fori_loop(0,ITERS,advance,start)
    for h in range(heads):
        car=dot3(a[h],sum_ref[h],1,0)
        fin_ref[h,0]=a[h]; fin_ref[h,1]=car
        rows=slice(h*HD,(h+1)*HD)
        ctx_ref[rows,:]=(dot(low(car),k1_ref[h,0],0,0)+conv_ref[rows,:].astype(F32)).astype(BF)

def back_marks_body(g_ref,k2_ref,peak_ref,hist_ref,fin_ref,k1_ref,sum_ref,v_ref,dsum_ref,dk2_ref,dinv_ref,dtap_ref,pad_ref,gst_ref):
    heads=k2_ref.shape[0]
    length=g_ref.shape[1]
    ident=eye()
    dinv_ref[...]=jnp.zeros(dinv_ref.shape,F32)
    dtap_ref[...]=jnp.zeros(dtap_ref.shape,F32)
    k2p=[parts(k2_ref[h]) for h in range(heads)]
    da=[]
    for h in range(heads):
        rows=slice(h*HD,(h+1)*HD)
        dcar=dot(k1_ref[h,0],g_ref[rows,:],1,1)
        dp_=parts(dcar)
        da.append(dot3(dp_,sum_ref[h],1,1))
        dsum_ref[h]=dot3(fin_ref[h,0],dp_,0,0)
    zero=jnp.zeros((LANDMARKS,LANDMARKS),F32)
    def retreat(done,carry):
        step=ITERS-1-done
        da,dk2=carry
        nxt=[]; out=[]
        for h in range(heads):
            A=parts(hist_ref[h,step,0]); P=hist_ref[h,step,1]; T2=hist_ref[h,step,2]; T3=hist_ref[h,step,3]
            Pp=parts(P); D=parts(da[h])
            dT3=0.25*dot3(A,D,0,0)
            dAn=0.25*dot3(D,T3,1,1)
            d3=parts(dT3)
            dT2=-dot3(Pp,d3,0,0)
            d2=parts(dT2)
            dP=-dot3(d3,T2,1,1)-dot3(d2,7.0*ident-P,1,1)+dot3(Pp,d2,0,0)
            dPp=parts(dP)
            out.append(dk2[h]+dot3(dPp,A,1,1))
            nxt.append(dAn+dot3(k2p[h],dPp,0,0))
        return tuple(nxt),tuple(out)
    da,dk2=lax.fori_loop(0,ITERS,retreat,(tuple(da),(zero,)*heads))
    for h in range(heads):
        inv=1.0/peak_ref[h:h+1,0:1]
        dk2_ref[h]=dk2[h]+da[h].T*inv
        prod=da[h]*k2_ref[h].T
        tot=jnp.sum(jnp.sum(prod,axis=0,keepdims=True),axis=1,keepdims=True)
        dinv_ref[h:h+1,:]=jnp.broadcast_to(tot,(1,128))
    r=lax.broadcasted_iota(jnp.int32,(SPAN,SPAN),0)
    c=lax.broadcasted_iota(jnp.int32,(SPAN,SPAN),1)
    flip=jnp.where(r+c==SPAN-1,1.0,0.0).astype(BF)
    for h in range(heads):
        wins=windows(pad_ref,v_ref[h,0],length)
        for b in range(length//SPAN):
            gst_ref[b*HD:(b+1)*HD,:]=g_ref[h*HD:(h+1)*HD,b*SPAN:(b+1)*SPAN]
        m=dot(low(dot(gst_ref[...],flip,1,0)),wins,0,0)
        m=pltpu.roll(m,0,1,stride=1,stride_axis=0)
        s=jnp.sum(m,axis=0,keepdims=True)
        dtap_ref[h:h+1,:]=s

def back_body(save_ref,g_ref,marks_ref,sum_ref,fin_ref,dsum_ref,taps_ref,dqkv_ref,dmarks_ref,pad_ref):
    length=g_ref.shape[1]
    g=g_ref[...]
    car=low(fin_ref[0,1]); dsum=dsum_ref[0]
    k1=save_ref[0,0].astype(F32)
    dk1=dot(car,g,1,0)
    ds1=low(k1*(dk1-jnp.sum(k1*dk1,axis=0,keepdims=True)))
    dqkv_ref[0]=low(dot(low(marks_ref[0,1]),ds1,0,0))
    dmarks_ref[0,1]=dot(ds1,save_ref[0,2],1,1)
    k3=save_ref[0,1]
    dl=low(dsum)
    delta=jnp.sum(dsum*sum_ref[0],axis=1,keepdims=True)
    ds3=low(k3.astype(F32)*(dot(dl,save_ref[0,4],1,0)-delta))
    dqkv_ref[1]=low(dot(low(marks_ref[0,0]),ds3,0,0))
    dmarks_ref[0,0]=dot(ds3,save_ref[0,3],1,1)
    wins=windows(pad_ref,g,length)
    out=dot(wins,low(band(taps_ref[0,1:2,:])),1,1)
    dv=dot(dl,k3,0,0)
    for b in range(length//SPAN):
        dqkv_ref[2,:,b*SPAN:(b+1)*SPAN]=(dv[:,b*SPAN:(b+1)*SPAN]+out[b*HD:(b+1)*HD,:]).astype(BF)

def close_body(k2_ref,dk2_ref,own_ref,marks_ref,dmarks_ref,dqkv_ref,out_ref):
    heads=k2_ref.shape[0]
    length=out_ref.shape[1]
    width=heads*HD
    factor=HD**-0.25
    seg=segments(length)
    scale=factor/(length//LANDMARKS)
    grads=[[None]*heads for _ in range(2)]
    for h in range(heads):
        k2=k2_ref[h]
        sums=jnp.sum(k2,axis=0,keepdims=True)
        hit=jnp.where(sums==jnp.max(sums,axis=1,keepdims=True),1.0,0.0)
        hit=hit*(1.0/jnp.sum(hit,axis=1,keepdims=True))
        dk2=dk2_ref[h]+hit*own_ref[h:h+1,0:1]
        ds2=k2*(dk2-jnp.sum(k2*dk2,axis=1,keepdims=True))
        dp=parts(ds2)
        grads[0][h]=((dmarks_ref[h,0]+dot3(dp,marks_ref[h,1],1,0))*scale).T
        grads[1][h]=((dmarks_ref[h,1]+dot3(dp,marks_ref[h,0],0,0))*scale).T
    dh,dl=parts(jnp.concatenate(grads[0]+grads[1],axis=0))
    spread=dot(dh,seg,1,0)+dot(dl,seg,1,0)
    for j in range(2):
        rows=slice(j*width,(j+1)*width)
        out_ref[rows,:]=(dqkv_ref[j].astype(F32)*factor+spread[rows,:]).astype(BF)
    out_ref[2*width:3*width,:]=dqkv_ref[2]
    if out_ref.shape[0]>3*width:
        out_ref[3*width:,:]=jnp.zeros((out_ref.shape[0]-3*width,length),BF)

def tap_rows(conv):
    _,count=conv.shape
    width=SPAN+2*REACH
    left=REACH-count//2
    pad=((0,0),(left,width-left-count))
    return jnp.stack([jnp.pad(conv,pad),jnp.pad(conv[:,::-1],pad)],axis=1)

VM=pl.BlockSpec(memory_space=pltpu.VMEM)
def sds(shape,dt=F32): return jax.ShapeDtypeStruct(shape,dt)
LIM=12*2**20
def params(): return pltpu.CompilerParams(vmem_limit_bytes=LIM)

def marks_call(qkv,heads):
    n=qkv.shape[2]
    return pl.pallas_call(marks_body,out_shape=(sds((heads,2,LANDMARKS,HD)),sds((heads,LANDMARKS,LANDMARKS)),sds((8,128))),
        in_specs=[pl.BlockSpec((2,heads*HD,n),lambda i:(0,0,0))],grid=(1,),
        out_specs=(pl.BlockSpec((heads,2,LANDMARKS,HD),lambda i:(0,0,0,0)),pl.BlockSpec((heads,LANDMARKS,LANDMARKS),lambda i:(0,0,0)),pl.BlockSpec((8,128),lambda i:(0,0))),
        name="marks",compiler_params=params())(qkv)

def fixed(shape,*at):
    return pl.BlockSpec(shape,lambda i:at)

def full(a):
    return fixed(a.shape,*(0,)*len(a.shape))

def out_full(*shapes):
    return tuple(full(x) for x in shapes)

def each(shape,spot):
    return pl.BlockSpec(shape,lambda h:tuple(h if d==spot else 0 for d in range(len(shape))))

def kernels_call(qkv,marks,taps,heads):
    n=qkv.shape[2]
    return pl.pallas_call(kernels_body,grid=(heads,),
        in_specs=[each((3,HD,n),1),each((1,2,LANDMARKS,HD),0),each((1,2,taps.shape[2]),0)],
        out_specs=(each((1,5,HD,n),0),each((1,LANDMARKS,HD),0),each((HD,n),0)),
        out_shape=(sds((heads,5,HD,n),BF),sds((heads,LANDMARKS,HD)),sds((heads*HD,n),BF)),
        scratch_shapes=[pltpu.VMEM((HD,n+2*REACH),BF)],name="kernels",compiler_params=params())(qkv,marks,taps)

def mix_call(k2,peak,sums,save,conv,heads):
    n=save.shape[3]
    outs=(sds((heads*HD,n),BF),sds((heads,ITERS,4,LANDMARKS,LANDMARKS)),sds((heads,2,LANDMARKS,LANDMARKS)))
    return pl.pallas_call(mix_body,grid=(1,),
        in_specs=[full(k2),full(peak),full(sums),fixed((heads,1,HD,n),0,0,0,0),full(conv)],
        out_specs=out_full(*outs),out_shape=outs,name="mix",compiler_params=params())(k2,peak,sums,save,conv)

def back_marks_call(g,k2,peak,hist,fin,save,sums,heads):
    n=g.shape[1]
    args=(g,k2,peak,hist,fin)
    outs=(sds((heads,LANDMARKS,HD)),sds((heads,LANDMARKS,LANDMARKS)),sds((8,128)),sds((8,SPAN+2*REACH)))
    return pl.pallas_call(back_marks_body,grid=(1,),
        in_specs=[full(a) for a in args]+[fixed((heads,1,HD,n),0,0,0,0),full(sums),fixed((heads,1,HD,n),0,4,0,0)],
        out_specs=out_full(*outs),out_shape=outs,
        scratch_shapes=[pltpu.VMEM((HD,n+2*REACH),BF),pltpu.VMEM((n//SPAN*HD,SPAN),BF)],
        name="back_marks",compiler_params=params())(*args,save,sums,save)

def back_call(save,g,marks,sums,fin,dsum,taps,heads):
    n=g.shape[1]
    sq=lambda: each((1,LANDMARKS,HD),0)
    two=lambda: each((1,2,LANDMARKS,HD),0)
    return pl.pallas_call(back_body,grid=(heads,),
        in_specs=[each((1,5,HD,n),0),each((HD,n),0),two(),sq(),two(),sq(),each((1,2,taps.shape[2]),0)],
        out_specs=(each((3,HD,n),1),two()),
        out_shape=(sds((3,heads*HD,n),BF),sds((heads,2,LANDMARKS,HD))),
        scratch_shapes=[pltpu.VMEM((HD,n+2*REACH),BF)],name="back",compiler_params=params())(save,g,marks,sums,fin,dsum,taps)

def close_call(k2,dk2,own,marks,dmarks,dqkv,rows):
    n=dqkv.shape[2]
    return pl.pallas_call(close_body,in_specs=[VM]*6,out_specs=VM,out_shape=sds((rows,n),BF),
        name="close",compiler_params=params())(k2,dk2,own,marks,dmarks,dqkv)

def final_body(grad_ref,own_ref,near_ref,far_ref,out_ref):
    out_ref[...]=grad_ref[...]+own_ref[...].astype(F32)+near_ref[...].astype(F32)+far_ref[...].astype(F32)

def final_call(grad,own,near,far):
    rows,width=grad.shape
    step=rows//4
    block=pl.BlockSpec((step,width),lambda i:(i,0))
    return pl.pallas_call(final_body,grid=(4,),in_specs=[block]*4,out_specs=block,out_shape=sds(grad.shape),
        name="final",compiler_params=params())(grad,own,near,far)


def xor_pairs(size, bit):
    return [(i, i ^ bit) for i in range(size)]


def xor_swap(value, axis, bit):
    return lax.ppermute(value, axis, xor_pairs(lax.axis_size(axis), bit))


def power_of_two(size):
    return size & (size - 1) == 0


def everywhere(value, axis, combine, plain):
    size = lax.axis_size(axis)
    if not power_of_two(size):
        return plain(value, axis)
    bit = 1
    while bit < size:
        far = xor_swap(value, axis, bit)
        value = combine(value, far)
        bit *= 2
    return value


def sum_everywhere(value, axis):
    return everywhere(value, axis, jnp.add, lax.psum)


def gather_near(value):
    far = xor_swap(value, "tensor", 2)
    near = xor_swap(value, "tensor", 1)
    last = xor_swap(far, "tensor", 1)
    return jnp.concatenate([value, near, far, last], axis=0)


def scatter_near(value):
    rows = value.shape[0] // 4
    block = lambda j: value[j * rows : (j + 1) * rows]
    last = xor_swap(block(3), "tensor", 1)
    sent = (block(2).astype(F32) + last.astype(F32)).astype(BF)
    far = xor_swap(sent, "tensor", 2)
    near = xor_swap(block(1), "tensor", 1)
    return block(0), near, far


def gather_pair(value):
    return jnp.concatenate([value, xor_swap(value, "tensor", 1)], axis=0)


def product_scattered(spec, value, weight):
    half = value.shape[0] // 2
    far = xor_swap(mul(spec, value[half:], weight, BF), "tensor", 1)
    return mul(spec, value[:half], weight) + far.astype(F32)


def gather_rows(value):
    size = lax.axis_size("fsdp")
    if size != 8:
        return lax.all_gather(value, "fsdp", axis=0)
    place = lax.axis_index("fsdp")
    width = value.shape[1] // 2
    left, right = value[:, :width], value[:, width:]
    right = jnp.stack([right, xor_swap(right, "fsdp", 1)])
    left = jnp.stack([left] + [xor_swap(left, "fsdp", k) for k in (2, 4, 6)])
    rights = [right]
    for k in (2, 4, 6):
        rights.append(xor_swap(right, "fsdp", k))
    right = jnp.stack(rights)
    left = jnp.stack([left, xor_swap(left, "fsdp", 1)], axis=1)

    def ordered(both):
        flat = both.reshape(size, *both.shape[2:])
        return jnp.concatenate(
            [lax.dynamic_slice_in_dim(flat, place ^ k, 1, 0) for k in range(size)], axis=0
        )

    return jnp.concatenate([ordered(left), ordered(right)], axis=2)


def reorder(value, axis):
    place = lax.axis_index("tensor")
    rows = value.shape[axis] // 4
    return jnp.concatenate(
        [lax.dynamic_slice_in_dim(value, (place ^ j) * rows, rows, axis) for j in range(4)], axis=axis
    )


def sum_at_owner(values, rows):
    count = lax.axis_size("fsdp")
    if count % 2:
        tiles = jnp.concatenate(values, axis=1).reshape(count, rows, -1)
        arrived = lax.all_to_all(tiles, "fsdp", split_axis=0, concat_axis=0, tiled=True)
        return arrived.astype(F32).sum(axis=0)
    side = lax.axis_index("fsdp") % 2
    pairs = []
    for value in values:
        tiles = value.reshape(count // 2, 2, rows, value.shape[1])
        sent = lax.dynamic_index_in_dim(tiles, 1 - side, 1, keepdims=False)
        got = xor_swap(sent, "fsdp", 1)
        kept = lax.dynamic_index_in_dim(tiles, side, 1, keepdims=False)
        pairs.append((kept.astype(F32) + got.astype(F32)).astype(BF))
    groups = [list(range(at, count, 2)) for at in range(2)]
    pair = pairs[0] if len(pairs) == 1 else jnp.concatenate(pairs, axis=2)
    arrived = lax.all_to_all(
        pair, "fsdp", split_axis=0, concat_axis=0, tiled=True, axis_index_groups=groups
    )
    return arrived.astype(F32).sum(axis=0)


def gelu_both(value):
    scale = (2.0 / jnp.pi) ** 0.5
    square = value * value
    bent = jnp.tanh(value * (scale + (scale * 0.044715) * square))
    half = 0.5 + 0.5 * bent
    slope = half + (0.5 * value) * (1.0 - bent * bent) * (scale + (3.0 * 0.044715 * scale) * square)
    return value * half, slope


def norm_forward(rows, gain, shift):
    center = rows - jnp.mean(rows, axis=-1, keepdims=True)
    spread = jnp.mean(center * center, axis=-1, keepdims=True)
    factor = lax.rsqrt(spread + 1e-05)
    normed = center * factor
    return (normed * gain + shift, normed, factor)


def norm_backward(cotan, normed, factor, gain):
    scaled = cotan * gain
    return factor * (
        scaled
        - jnp.mean(scaled, axis=-1, keepdims=True)
        - normed * jnp.mean(scaled * normed, axis=-1, keepdims=True)
    )


def norm_params(cotan, normed):
    return (jnp.sum(cotan * normed, axis=0), jnp.sum(cotan, axis=0))


def mul(spec, a, b, kind=F32):
    return jnp.einsum(spec, a, b, preferred_element_type=F32).astype(kind)


def shards(
    inputs,
    qkv_weight,
    out_weight,
    conv_weight,
    up_weight,
    down_weight,
    mix_gain,
    mix_bias,
    feed_gain,
    feed_bias,
    out_grad,
):
    place = lax.axis_index("tensor")
    columns = qkv_weight.shape[2]
    heads = columns // HD
    units = up_weight.shape[1]
    share = qkv_weight.shape[1]
    gathered_in = reorder(gather_near(inputs.astype(BF)), 0)
    direct = jnp.concatenate([qkv_weight[0], qkv_weight[1], qkv_weight[2], out_weight.T], axis=1)
    direct = gather_rows(direct)
    direct = direct.reshape(-1, direct.shape[2])
    w_qkv = direct[:, : 3 * columns]
    w_out = direct[:, 3 * columns :]
    packed = jnp.concatenate([up_weight, down_weight.T], axis=1)
    members = lax.axis_size("fsdp")
    groups = [[f * 4 + y * 2 + c for y in range(2) for f in range(members)] for c in range(2)]
    w_rest = lax.all_gather(packed, ("fsdp", "tensor"), axis=0, axis_index_groups=groups)
    w_rest = w_rest.reshape(2, -1, 2 * units)
    w_up = jnp.concatenate([w_rest[0, :, :units], w_rest[1, :, :units]], axis=1)
    w_down = jnp.concatenate([w_rest[0, :, units:], w_rest[1, :, units:]], axis=1)
    half = place // 2
    own_units = lambda value: lax.dynamic_slice_in_dim(value, half * units, units, 1)
    far_units = lambda value: lax.dynamic_slice_in_dim(value, (1 - half) * units, units, 1)
    qkv = mul("nd,dc->cn", gathered_in, w_qkv).reshape(3, columns, -1)
    conv_local = lax.dynamic_slice_in_dim(conv_weight, place * heads, heads, 0)
    taps = tap_rows(conv_local)
    marks, k2, peak_local = marks_call(qkv, heads)
    peak = everywhere(peak_local, "fsdp", jnp.maximum, lax.pmax)
    save, summary, conv = kernels_call(qkv, marks, taps, heads)
    context, hist, fin = mix_call(k2, peak, summary, save, conv, heads)
    context_own = reorder(context, 1)
    own, near, far = scatter_near(mul("cn,dc->nd", context_own, w_out, BF))
    attended = own.astype(F32) + near.astype(F32) + far.astype(F32)
    mixed_rows, normed_mix, factor_mix = norm_forward(inputs + attended, mix_gain, mix_bias)
    mixed_low = gather_pair(mixed_rows.astype(BF))
    act, slope = gelu_both(mul("nd,df->nf", mixed_low, w_up))
    act, slope = act.astype(BF), slope.astype(BF)
    fed = product_scattered("nf,df->nd", act, w_down)
    output, normed_feed, factor_feed = norm_forward(mixed_rows + fed, feed_gain, feed_bias)
    grad_feed = norm_backward(out_grad, normed_feed, factor_feed, feed_gain)
    feed_gain_part, feed_bias_part = norm_params(out_grad, normed_feed)
    grad_down = gather_pair(grad_feed.astype(BF))
    grad_up = (mul("nd,df->nf", grad_down, w_down) * slope.astype(F32)).astype(BF)
    grad_mixed_rows = grad_feed + product_scattered("nf,df->nd", grad_up, w_up)
    down_pair = mul("nd,nf->df", grad_down, act, BF)
    down_pair = sum_at_owner([down_pair], share)
    far = xor_swap(far_units(down_pair).astype(BF), "tensor", 2)
    down_share = (own_units(down_pair) + far.astype(F32)).T
    grad_mix = norm_backward(grad_mixed_rows, normed_mix, factor_mix, mix_gain)
    mix_gain_part, mix_bias_part = norm_params(grad_mixed_rows, normed_mix)
    grad_attended = gather_near(grad_mix.astype(BF))
    far = mul("nd,nf->df", mixed_low, far_units(grad_up), BF)
    far = xor_swap(far, "tensor", 2)
    up_sum = mul("nd,nf->df", mixed_low, own_units(grad_up)) + far.astype(F32)
    extra = jnp.zeros((-columns % 128, context_own.shape[1]), BF)
    out_sum = mul("nd,cn->dc", grad_attended, jnp.concatenate([context_own, extra]), BF)
    up_share = sum_at_owner([up_sum.astype(BF), out_sum], share)
    out_share = up_share[:, units : units + columns].T
    up_share = up_share[:, :units]
    grad_context = reorder(mul("nd,dc->cn", grad_attended, w_out, BF), 1)
    dsum, dk2, dinv, dtap = back_marks_call(grad_context, k2, peak, hist, fin, save, summary, heads)
    first = SPAN - 1 + REACH - conv_weight.shape[1] // 2
    dtap = dtap[:, first : first + 128]
    norm_stack = jnp.stack([mix_gain_part, mix_bias_part, feed_gain_part, feed_bias_part])
    norm_rows = norm_stack.reshape(-1, 128)
    total = sum_everywhere(jnp.concatenate([dinv, dtap, norm_rows], axis=0), "fsdp")
    own = jnp.where(peak_local == peak, -total[:8] / (peak * peak), 0.0)
    dqkv, dmarks = back_call(save, grad_context, marks, summary, fin, dsum, taps, heads)
    padded = 3 * columns + (-3 * columns) % 128
    grad_qkv = close_call(k2, dk2, own, marks, dmarks, dqkv, padded)
    conv_full = lax.dynamic_update_slice_in_dim(
        jnp.zeros((conv_weight.shape[0], 128), F32), total[8 : 8 + heads], place * heads, 0
    )
    total = sum_everywhere(jnp.concatenate([conv_full, total[16:]], axis=0), "tensor")
    conv_grad = total[: conv_weight.shape[0], : conv_weight.shape[1]]
    norm_sum = total[conv_weight.shape[0] :].reshape(norm_stack.shape)
    qkv_grad = mul("nd,cn->dc", gathered_in, grad_qkv, BF)
    qkv_share = sum_at_owner([qkv_grad], share)
    qkv_share = jnp.moveaxis(qkv_share[:, : 3 * columns].reshape(share, 3, columns), 1, 0)
    input_part = reorder(mul("cn,dc->nd", grad_qkv, direct[:, :padded], BF), 0)
    input_grad = final_call(grad_mix, *scatter_near(input_part))
    return (
        output,
        input_grad,
        qkv_share,
        out_share,
        conv_grad,
        up_share,
        down_share,
        norm_sum[0],
        norm_sum[1],
        norm_sum[2],
        norm_sum[3],
    )


def solution(mesh):
    rows = P(("fsdp", "tensor"), None)
    cross = P("tensor", "fsdp")
    stacked = P(None, "fsdp", "tensor")

    return jax.shard_map(
        shards,
        mesh=mesh,
        in_specs=(rows, stacked, cross, P(), P("fsdp", "tensor"), cross, P(), P(), P(), P(), rows),
        out_specs=(rows, rows, stacked, cross, P(), P("fsdp", "tensor"), cross, P(), P(), P(), P()),
        check_vma=False,
    )
```
